32 devices in a mesh: dp: 8 (over z, y), shard: 4 (over x, core).
Axes of the slice: x: 2, y: 2, z: 4, core: 2. Of those that a mesh axis runs over, the one named last changes fastest.
Arguments:
- hidden_acts: bfloat16 [8, 128, 8192], P('dp', None, 'shard'), may hold values from -6 to 6
- out_grad: bfloat16 [8, 128, 1024], P('dp'), may hold values from -0.0546875 to 0.0546875
- token_ids: int32 [8, 128], P('dp'), may hold values from 0 to 255999, as said below
- trigger: int32 [8, 512], P('dp', 'shard'), may hold values 0 or 1
- stale: bfloat16 [8, 8192, 1024], P('dp', 'shard'), may hold values from -0.5 to 0.5
- aggregate_prev: float32 [4, 2048, 1024], P('shard', 'dp'), may hold values from -12 to 12
Outputs:
- aggregate: float32 [4, 2048, 1024], P('shard', 'dp')
- update: float32 [4, 2048, 1024], P('shard', 'dp')
- triggered: float32 [], replicated
The draws below stay inside these ranges and needn't reach their ends.
Inputs may be any that keep to these rules, and one draw needn't show every extreme that they name: `token_ids`: id 0 marks padding and stands only after all of a worker's other tokens; at least half of each worker's 128 tokens are not padding.
All inputs are finite; a program needn't handle non-finite values. No bound on the sum of `trigger` on one device may be relied on, other than what follows from the above.
Results may differ from the reference program's by a relative error of at most 0.00051.
Values may be sent and summed in bfloat16 or wider, within the bound.
No kernel may reach another device: no remote copies, remote signals or barrier semaphores. Data moves between devices by JAX's collectives and lax.ppermute only.
A program may use at most 64 MiB of HBM per device.

```python
import math
import jax
import jax.numpy as jnp
from jax import lax

COLS = 1024
HID = 8192
VOCAB = 256000
BLOCK = 16
TOK_DEV = 128
WORKERS = 8
N_SHARD = 4


def draw_token_ids(key, part):
    length_key = jax.random.fold_in(key, 11)
    id_key = jax.random.fold_in(key, 23)
    lengths = jax.random.randint(length_key, (WORKERS, 1), TOK_DEV // 2, TOK_DEV + 1)
    values = jax.random.randint(id_key, (WORKERS, TOK_DEV), 1, VOCAB)
    position = jnp.arange(TOK_DEV)[None, :]
    return jnp.where(position < lengths, values, 0).astype(jnp.int32)


def draw_aggregate_prev(key, part):
    array_shape = (N_SHARD, HID // N_SHARD, COLS)
    row_index = jnp.arange(HID, dtype=jnp.float32).reshape(N_SHARD, HID // N_SHARD, 1)
    scales = jnp.exp(jnp.log(3.0) * row_index / HID)
    values = jnp.clip(jax.random.normal(key, array_shape, jnp.float32), -4.0, 4.0)
    return (values * scales).astype(jnp.float32)


def draw_stale(key, part):
    common_key = jax.random.fold_in(key, 31)
    jitter_key = jax.random.fold_in(key, 47)
    column_key = jax.random.fold_in(key, 59)
    shard_rows = HID // N_SHARD
    row_place = (jnp.arange(HID) % shard_rows).astype(jnp.float32) / shard_rows
    row_amp = jnp.exp(0.5 * jnp.log(3.0) * row_place)[:, None]
    column_amp = jnp.exp(jax.random.uniform(column_key, (1, COLS), jnp.float32, math.log(0.5), math.log(1.5)))
    common = 0.057 * jnp.clip(jax.random.normal(common_key, (HID, COLS), jnp.float32), -3.0, 3.0)
    jitter = 0.01 * jnp.clip(jax.random.normal(jitter_key, (WORKERS, HID, COLS), jnp.float32), -3.0, 3.0)
    shared = common * row_amp * column_amp
    return (shared[None, :, :] + jitter).astype(jnp.bfloat16)


def set_ends(values, own_key, least, largest):
    extent = values.shape
    index_at = [jax.random.randint(jax.random.fold_in(own_key, axis), (), 0, extent[axis]) for axis in range(len(extent))]
    values = values.at[tuple(index_at)].set(least)
    longest = extent.index(max(extent))
    index_at[longest] = (index_at[longest] + 1) % extent[longest]
    return values.at[tuple(index_at)].set(largest)


def levels(rng, extent, shards, low, largest):
    loudness = 1.0
    for dim, blocks in shards:
        heights = jax.random.uniform(jax.random.fold_in(jax.random.fold_in(rng, 6), dim), (blocks,), jnp.float32, low / len(shards), largest / len(shards))
        loudness = loudness * jnp.repeat(jnp.exp(heights), extent[dim] // blocks).reshape((-1,) + (1,) * (len(extent) - 1 - dim))
    return loudness


def scatter_about(stream_key, dims, width, bound, split=(), held_as=jnp.bfloat16):
    result = jax.random.normal(stream_key, dims, jnp.float32) * width
    if len(split) > 0:
        result = levels(stream_key, dims, split, -0.22, 0.18) * result
    return jnp.clip(result, min=-bound, max=bound).astype(held_as)


def setup_inputs(seed: int = 0) -> dict:
    key_of = jax.random.split(jax.random.key(seed), 7)
    return {
        "hidden_acts": scatter_about(key_of[0], (WORKERS, TOK_DEV, HID), 1.0, 6.0, ((0, 8), (2, 4))),
        "out_grad": scatter_about(key_of[1], (WORKERS, TOK_DEV, COLS), (100 * TOK_DEV) ** -0.5, 0.0546875, ((0, 8),)),
        "token_ids": draw_token_ids(jax.random.fold_in(key_of[6], 71), 0),
        "trigger": set_ends((jax.random.randint(key_of[3], (WORKERS, HID // BLOCK), 0, 2) < 1).astype(jnp.int32), jax.random.fold_in(key_of[3], 1), 0, 1),
        "stale": draw_stale(jax.random.fold_in(key_of[6], 71), 0),
        "aggregate_prev": draw_aggregate_prev(jax.random.fold_in(key_of[6], 71), 0),
    }


clip_ratio = 0.25
epsilon = 1e-06

def reference(hidden_acts, out_grad, token_ids, trigger, stale, aggregate_prev):
    real_mask = (token_ids != 0).astype(jnp.bfloat16)
    masked = out_grad * real_mask[:, :, None]

    def accumulate(running, worker_items):
        hidden, grad_out, flags, stale_rows = worker_items
        gradient = lax.dot_general(hidden, grad_out, (((0,), (0,)), ((), ())), preferred_element_type=jnp.float32)
        row_flags = jnp.repeat(flags, BLOCK).astype(jnp.float32)[:, None]
        delta = (row_flags * (gradient - stale_rows.astype(jnp.float32))).astype(jnp.bfloat16)
        delta = lax.optimization_barrier(delta)
        return (running + delta.astype(jnp.float32), None)
    start_sum = jnp.zeros((HID, COLS), jnp.float32)
    summed, unused = lax.scan(accumulate, start_sum, (hidden_acts, masked, trigger, stale))
    aggregate = aggregate_prev + summed.reshape(N_SHARD, HID // N_SHARD, COLS)
    triggered = jnp.sum(trigger.astype(jnp.float32))
    square_total = jnp.sum(aggregate * aggregate)
    limit = clip_ratio * jnp.sqrt(jnp.asarray(HID * COLS, jnp.float32))
    clip_factor = jnp.minimum(1.0, limit / jnp.sqrt(square_total + epsilon))
    return (aggregate, aggregate * clip_factor, triggered)
```

```python
import jax
import jax.numpy as jnp
from jax import lax
from jax.experimental import pallas as pl
from jax.experimental.pallas import tpu as pltpu
from jax.sharding import PartitionSpec as P

COLS = 1024
HID = 8192
BLOCK = 16
clip_ratio = 0.25
epsilon = 1e-06
MIB = 1 << 20
STAGES = 3
ROUNDING = 4.8e-4
F32, BF16 = jnp.float32, jnp.bfloat16
VMEM = pl.BlockSpec(memory_space=pltpu.VMEM)
SMEM = pl.BlockSpec(memory_space=pltpu.SMEM)
HBM = pl.BlockSpec(memory_space=pltpu.HBM)

A0, A1, A, B = (0, 7), (7, 6), (0, 13), (13, 3)
RAW = (
    ("y6a", 1, ((6, A0),)),
    ("y4a", 1, ((4, A0),)),
    ("zb0", 2, ((5, B), (4, B))),
    ("y6b", 1, ((6, A1),)),
    ("zb1", 2, ((1, B), (0, B))),
    ("y4b", 1, ((4, A1),)),
    ("y2a", 1, ((2, A0),)),
    ("y2b", 1, ((2, A1),)),
    ("y0", 1, ((0, A),)),
)
OWN = ((6, A0), (5, B), (4, A0), (4, B), (6, A1), (4, A1), (1, B), (2, A0), (2, A1), (0, A), (0, B))
SUMS = (
    ("near0", 2, (6, A0), (("y6a", 0),), 0),
    ("pairb5", 1, (5, B), (("zb0", 0),), 0),
    ("quad0", 4, (4, A0), (("y4a", 0), ("near0", 0)), 1),
    ("near1", 2, (6, A1), (("y6b", 0),), 0),
    ("pairb1", 1, (1, B), (("zb1", 0),), 2),
    ("quadb", 4, (4, B), (("zb0", 1), ("pairb5", 0)), 1),
    ("quad1", 4, (4, A1), (("y4b", 0), ("near1", 0)), 1),
    ("last0", 2, (2, A0), (("y2a", 0),), 2),
    ("last1", 2, (2, A1), (("y2b", 0),), 2),
)
FINAL = (
    (A0, (0, A), 0, (("y0", 0), ("last0", 0), ("quad0", 0))),
    (A1, (0, A), 7, (("y0", 7), ("last1", 0), ("quad1", 0))),
    (B, (0, B), 0, (("zb1", 3), ("pairb1", 0), ("quadb", 0))),
)


def fold(x):
    sq = x * x
    total = jnp.zeros((8, 128), F32)
    for c in range(0, x.shape[1], 128):
        for r in range(0, x.shape[0], 8):
            total = total + sq[r : r + 8, c : c + 128]
    return total


def deltas(me, trig, tok, acts, og, stale, messages, chunk, limit):
    tokens, width = og.shape[1], og.shape[2]
    unit = chunk // 16
    pieces = [(i, m, r) for i, message in enumerate(messages) for m, r in message]
    masks = list(dict.fromkeys(m for _, m, _ in pieces))
    heights = [sum(r[1] for _, r in message) * unit for message in messages]
    total = sum(heights)
    n_out = len(messages)

    def kernel(me_ref, trig_ref, tok_ref, acts_hbm, og_hbm, stale_hbm, *refs):
        outs = refs[:n_out]
        acts_buf, og_buf, stale_buf, sem = refs[n_out:]
        start = {m: pl.multiple_of((me_ref[0] ^ m) * chunk, chunk) for m in masks}
        og_copy = pltpu.make_async_copy(og_hbm.at[0], og_buf, sem.at[0])
        act_copies, stale_copies = {}, []
        for j, m in enumerate(masks):
            act_copies[m] = pltpu.make_async_copy(
                acts_hbm.at[0, :, pl.ds(start[m], chunk)], acts_buf.at[j], sem.at[1 + j]
            )
        at = 0
        for j, (_, m, (first, count)) in enumerate(pieces):
            rows = pl.ds(pl.multiple_of(start[m] + first * unit, unit), count * unit)
            stale_copies.append(
                pltpu.make_async_copy(
                    stale_hbm.at[0, rows, :], stale_buf.at[pl.ds(at, count * unit), :], sem.at[1 + len(masks) + j]
                )
            )
            at += count * unit
        act_copies[masks[0]].start()
        og_copy.start()
        begun = {masks[0]}
        for j, (_, m, _) in enumerate(pieces):
            if m not in begun:
                act_copies[m].start()
                begun.add(m)
            stale_copies[j].start()
        real = (tok_ref[...] != 0).astype(BF16)
        weights = {}
        at, offset, last = 0, 0, -1
        for j, (i, m, (first, count)) in enumerate(pieces):
            offset = 0 if i != last else offset
            last = i
            if m not in weights:
                act_copies[m].wait()
                weights[m] = acts_buf[masks.index(m)].T * real
            if j == 0:
                og_copy.wait()
            part = weights[m][first * unit : (first + count) * unit]
            gradient = jnp.dot(part, og_buf[...], preferred_element_type=F32)
            stale_copies[j].wait()
            for b in range(0, count * unit, BLOCK):
                flag = trig_ref[(start[m] + first * unit + b) // BLOCK].astype(F32)
                old = stale_buf[at + b : at + b + BLOCK, :].astype(F32)
                outs[i][offset + b : offset + b + BLOCK, :] = (flag * (gradient[b : b + BLOCK] - old)).astype(BF16)
            at += count * unit
            offset += count * unit

    return pl.pallas_call(
        kernel,
        out_shape=tuple(jax.ShapeDtypeStruct((h, width), BF16) for h in heights),
        in_specs=[SMEM, SMEM, VMEM] + [HBM] * 3,
        out_specs=tuple(VMEM for _ in messages),
        scratch_shapes=[
            pltpu.VMEM((len(masks), tokens, chunk), BF16),
            pltpu.VMEM((tokens, width), BF16),
            pltpu.VMEM((total, width), BF16),
            pltpu.SemaphoreType.DMA((1 + len(masks) + len(pieces),)),
        ],
        cost_estimate=pl.CostEstimate(
            flops=2 * tokens * total * width, bytes_accessed=total * width * 4, transcendentals=0
        ),
        compiler_params=pltpu.CompilerParams(vmem_limit_bytes=limit),
    )(me, trig, tok, acts, og, stale)


def add_round(parts, rows):
    width = parts[0][0].shape[1]

    def kernel(*refs):
        out, lost = refs[-2:]
        energy = jnp.zeros((8, 128), F32)
        for r in range(0, rows, BLOCK):
            total = jnp.zeros((BLOCK, width), F32)
            for ref, (_, at) in zip(refs, parts):
                total = total + ref[at + r : at + r + BLOCK, :].astype(F32)
            rounded = total.astype(BF16)
            out[r : r + BLOCK, :] = rounded
            energy = energy + fold(total - rounded.astype(F32))
        lost[...] = energy

    return pl.pallas_call(
        kernel,
        out_shape=(jax.ShapeDtypeStruct((rows, width), BF16), jax.ShapeDtypeStruct((8, 128), F32)),
        in_specs=[VMEM] * len(parts),
        out_specs=(VMEM, VMEM),
        cost_estimate=pl.CostEstimate(flops=rows * width * 6, bytes_accessed=rows * width * 6, transcendentals=0),
        compiler_params=pltpu.CompilerParams(vmem_limit_bytes=12 * MIB),
    )(*[x for x, _ in parts])


def finish(prev, groups, lost, trig):
    arrays = {id(x): x for _, addends in groups for x, _ in addends}
    keys = list(arrays)
    flat = [x for group in lost for x in group]
    n_arrays, n_lost = len(keys), len(flat)

    def kernel(trig_ref, prev_ref, *refs):
        lost_refs = list(refs[n_arrays : n_arrays + n_lost])
        agg, kept, sums, sem = refs[n_arrays + n_lost :]
        total = jnp.zeros((8, 128), F32)
        copies = []
        for g, ((first, rows), addends) in enumerate(groups):
            for r in range(0, rows, BLOCK):
                a = prev_ref[0, first + r : first + r + BLOCK, :]
                for x, at in addends:
                    a = a + refs[keys.index(id(x))][at + r : at + r + BLOCK, :].astype(F32)
                kept[0, first + r : first + r + BLOCK, :] = a
                total = total + fold(a)
            span = pl.ds(first, rows)
            copies.append(pltpu.make_async_copy(kept.at[:, span], agg.at[:, span], sem.at[g]))
            copies[-1].start()
        hits = trig_ref[...].astype(F32)
        row = lax.broadcasted_iota(jnp.int32, (8, 128), 0)
        lane = lax.broadcasted_iota(jnp.int32, (8, 128), 1)
        stacked = jnp.where(row == 0, jnp.sum(total, axis=0, keepdims=True), jnp.where(row == 1, hits, 0.0))
        for i, group in enumerate(lost):
            tile = sum(lost_refs.pop(0)[...] for _ in group)
            stacked = jnp.where(row == 2 + i, jnp.sum(tile, axis=0, keepdims=True), stacked)
        values = jnp.sum(stacked, axis=1, keepdims=True)
        line = jnp.sum(jnp.where(row == lane, values, 0.0), axis=0, keepdims=True)
        sums[...] = jnp.broadcast_to(line[None], sums.shape)
        for c in copies:
            c.wait()

    n = lax.axis_size("dp") * lax.axis_size("shard")
    whole = jax.ShapeDtypeStruct(prev.shape, F32)
    return pl.pallas_call(
        kernel,
        out_shape=(whole, whole, jax.ShapeDtypeStruct((n, 1, 128), F32)),
        in_specs=[VMEM] * (2 + n_arrays + n_lost),
        out_specs=(HBM, VMEM, VMEM),
        scratch_shapes=[pltpu.SemaphoreType.DMA((len(groups),))],
        compiler_params=pltpu.CompilerParams(vmem_limit_bytes=12 * MIB),
        name="finish",
    )(trig, prev, *arrays.values(), *flat)


def scale(agg, gathered):
    devices = gathered.shape[0]
    pieces = 4
    rows = agg.shape[1] // pieces

    def kernel(agg_ref, all_ref, out, hits, bad, buf, sem):
        table = all_ref[:, 0, :]
        s = jnp.sum(table, axis=0, keepdims=True)
        lane = lax.broadcasted_iota(jnp.int32, (1, 128), 1)
        pick = lambda x, where: jnp.sum(jnp.where(where, x, 0.0), axis=1, keepdims=True)
        square_total = pick(s, lane == 0)
        limit = clip_ratio * jnp.sqrt(jnp.full((1, 1), HID * COLS, F32))
        factor = jnp.minimum(1.0, limit / jnp.sqrt(square_total + epsilon))
        copies = []
        for p in range(pieces):
            span = pl.ds(p * rows, rows)
            buf[0, p * rows : (p + 1) * rows, :] = agg_ref[0, p * rows : (p + 1) * rows, :] * factor
            copies.append(pltpu.make_async_copy(buf.at[:, span], out.at[:, span], sem.at[p]))
            copies[-1].start()
        most = jnp.max(table, axis=0, keepdims=True)
        hits[...] = pick(s, lane == 1)
        roundings = (lane >= 2) & (lane < 2 + STAGES)
        room = (ROUNDING * ROUNDING / STAGES) * square_total
        over = (pick(s, roundings) > room) | (devices * pick(most, roundings) > 2.0 * room)
        bad[...] = over.astype(jnp.int32)
        for c in copies:
            c.wait()

    one = lambda t: jax.ShapeDtypeStruct((1, 1), t)
    return pl.pallas_call(
        kernel,
        out_shape=(jax.ShapeDtypeStruct(agg.shape, F32), one(F32), one(jnp.int32)),
        in_specs=[VMEM, VMEM],
        out_specs=(HBM, VMEM, VMEM),
        scratch_shapes=[pltpu.VMEM(agg.shape, F32), pltpu.SemaphoreType.DMA((pieces,))],
        compiler_params=pltpu.CompilerParams(vmem_limit_bytes=8 * MIB),
        name="scale",
    )(agg, gathered)


def local(*args):
    return step(*args)


def step(hidden_acts, out_grad, token_ids, trigger, stale, aggregate_prev):
    n = lax.axis_size("dp")
    chunk = aggregate_prev.shape[1]
    unit = chunk // 16
    me = lax.axis_index("dp").astype(jnp.int32).reshape(1)
    args = (me, trigger[0], token_ids, hidden_acts, out_grad, stale)

    def swap(x, mask):
        return lax.ppermute(x, "dp", [(i, i ^ mask) for i in range(n)])

    outgoing = [[(m ^ bit, rows) for m, rows in parts] for _, bit, parts in RAW]
    made = list(deltas(*args, outgoing[:1], chunk, 60 * 1024 * 1024))
    made += deltas(*args, outgoing[1:], chunk, 16 * MIB)
    got = {label: swap(x, bit) for (label, bit, _), x in zip(RAW, made)}
    own = dict(zip(OWN, deltas(*args, [[key] for key in OWN], chunk, 16 * MIB)))
    lost = [[] for _ in range(STAGES)]
    for label, bit, mine, others, group in SUMS:
        parts = [(own[mine], 0)] + [(got[name], k * mine[1][1] * unit) for name, k in others]
        total, energy = add_round(parts, mine[1][1] * unit)
        lost[group].append(energy)
        got[label] = swap(total, bit)
    groups = []
    for (first, count), mine, at, others in FINAL:
        addends = [(own[mine], at * unit)] + [(got[name], k * unit) for name, k in others]
        groups.append(((first * unit, count * unit), addends))
    agg, kept, sums = finish(aggregate_prev, groups, lost, trigger)
    everyone = lax.all_to_all(sums, ("dp", "shard"), 0, 0, tiled=True)
    update, hits, bad = scale(kept, everyone)

    def again(state):
        mine = deltas(*args, [[(m, (0, 16))] for m in range(n)], chunk, 24 * MIB)
        came = [mine[0]] + [lax.ppermute(mine[m], "dp", [(i, i ^ m) for i in range(n)]) for m in range(1, n)]
        new_agg, new_kept, new_sums = finish(aggregate_prev, [((0, chunk), [(x, 0) for x in came])], [], trigger)
        new_update, _, _ = scale(new_kept, lax.all_to_all(new_sums, ("dp", "shard"), 0, 0, tiled=True))
        return jnp.zeros((), jnp.int32), new_agg, new_update

    _, agg, update = lax.while_loop(lambda state: state[0] > 0, again, (bad[0, 0], agg, update))
    return agg, update, hits[0, 0]


def exact(hidden_acts, out_grad, token_ids, trigger, stale, aggregate_prev):
    masked = out_grad[0] * (token_ids[0] != 0).astype(BF16)[:, None]
    row_flags = jnp.repeat(trigger[0], BLOCK).astype(F32)[:, None]
    triggered = lax.psum(jnp.sum(trigger.astype(F32)), ("dp", "shard"))
    gradient = lax.dot_general(hidden_acts[0], masked, (((0,), (0,)), ((), ())), preferred_element_type=F32)
    delta = (row_flags * (gradient - stale[0].astype(F32))).astype(BF16)
    delta = delta.reshape(lax.axis_size("dp"), aggregate_prev.shape[1], stale.shape[2])
    received = lax.all_to_all(delta, "dp", split_axis=0, concat_axis=0, tiled=True)
    aggregate = aggregate_prev[0] + jnp.sum(received, axis=0, dtype=F32)
    square_total = lax.psum(jnp.sum(aggregate * aggregate), ("dp", "shard"))
    limit = clip_ratio * jnp.sqrt(jnp.asarray(HID * COLS, F32))
    factor = jnp.minimum(1.0, limit / jnp.sqrt(square_total + epsilon))
    return aggregate[None], (aggregate * factor)[None], triggered


def solution(mesh):
    staged = mesh.shape["dp"] == 8
    return jax.shard_map(
        local if staged else exact,
        mesh=mesh,
        in_specs=(
            P("dp", None, "shard"),
            P("dp", None, None),
            P("dp", None),
            P("dp", "shard"),
            P("dp", "shard", None),
            P("shard", "dp", None),
        ),
        out_specs=(P("shard", "dp", None), P("shard", "dp", None), P()),
        check_vma=False,
    )
```

```python
import jax
import jax.numpy as jnp
from jax import lax
from jax.experimental import pallas as pl
from jax.experimental.pallas import tpu as pltpu
from jax.sharding import PartitionSpec as P

COLS = 1024
HID = 8192
BLOCK = 16
clip_ratio = 0.25
epsilon = 1e-06
MIB = 1 << 20
PIECE = 64
STAGES = 3
ROUNDING = 4.8e-4
F32, BF16 = jnp.float32, jnp.bfloat16
VMEM = pl.BlockSpec(memory_space=pltpu.VMEM)
SMEM = pl.BlockSpec(memory_space=pltpu.SMEM)
HBM = pl.BlockSpec(memory_space=pltpu.HBM)

A0, A1, B = (0, 6), (6, 7), (13, 3)
RAW = (
    ("y6a", 1, ((6, A0),)),
    ("zb0", 2, ((5, B), (4, B))),
    ("y4a", 1, ((4, A0),)),
    ("y6b", 1, ((6, A1),)),
    ("zb1", 2, ((1, B), (0, B))),
    ("y4b", 1, ((4, A1),)),
    ("y2a", 1, ((2, A0),)),
    ("y2b", 1, ((2, A1),)),
    ("y0b", 1, ((0, A1),)),
    ("y0a", 1, ((0, A0),)),
)
FIRST = 3
OWN_EARLY = ((6, A0), (5, B), (4, A0), (6, A1))
OWN_LATE = ((4, B), (4, A1), (1, B), (2, A0), (2, A1), (0, A0), (0, A1), (0, B))
SUMS = (
    ("near0", 2, (6, A0), (("y6a", 0),), 0),
    ("pairb5", 1, (5, B), (("zb0", 0),), 0),
    ("quad0", 4, (4, A0), (("y4a", 0), ("near0", 0)), 1),
    ("near1", 2, (6, A1), (("y6b", 0),), 0),
    ("pairb1", 1, (1, B), (("zb1", 0),), 2),
    ("quadb", 4, (4, B), (("zb0", 1), ("pairb5", 0)), 1),
    ("quad1", 4, (4, A1), (("y4b", 0), ("near1", 0)), 1),
    ("last0", 2, (2, A0), (("y2a", 0),), 2),
    ("last1", 2, (2, A1), (("y2b", 0),), 2),
)
FINAL = (
    (B, (0, B), (("zb1", 1), ("pairb1", 0), ("quadb", 0))),
    (A1, (0, A1), (("y0b", 0), ("last1", 0), ("quad1", 0))),
)
LAST = ((A0, (0, A0), (("y0a", 0), ("last0", 0), ("quad0", 0))),)


def fold(x):
    sq = x * x
    total = jnp.zeros((8, 128), F32)
    for c in range(0, x.shape[1], 128):
        for r in range(0, x.shape[0], 8):
            total = total + sq[r : r + 8, c : c + 128]
    return total


def deltas(trig, tok, acts, og, stale, messages, chunk, limit):
    tokens, width = og.shape[1], og.shape[2]
    unit = chunk // 16
    pieces = [(i, m, r) for i, message in enumerate(messages) for m, r in message]
    masks = list(dict.fromkeys(m for _, m, _ in pieces))
    heights = [sum(r[1] for _, r in message) * unit for message in messages]
    total = sum(heights)
    n_out = len(messages)

    def kernel(trig_hbm, tok_hbm, acts_hbm, og_hbm, stale_hbm, *refs):
        outs = refs[:n_out]
        acts_buf, og_buf, stale_buf, tok_ref, trig_ref, small, sem = refs[n_out:]
        me = lax.axis_index("dp")
        start = {m: pl.multiple_of((me ^ m) * chunk, chunk) for m in masks}
        tok_copy = pltpu.make_async_copy(tok_hbm, tok_ref, small.at[0])
        trig_copy = pltpu.make_async_copy(trig_hbm, trig_ref, small.at[1])
        og_copy = pltpu.make_async_copy(og_hbm.at[0], og_buf, sem.at[0])
        act_copies, stale_copies = {}, []
        for j, m in enumerate(masks):
            act_copies[m] = pltpu.make_async_copy(
                acts_hbm.at[0, :, pl.ds(start[m], chunk)], acts_buf.at[j], sem.at[1 + j]
            )
        at = 0
        for j, (_, m, (first, count)) in enumerate(pieces):
            rows = pl.ds(pl.multiple_of(start[m] + first * unit, unit), count * unit)
            stale_copies.append(
                pltpu.make_async_copy(
                    stale_hbm.at[0, rows, :], stale_buf.at[pl.ds(at, count * unit), :], sem.at[1 + len(masks) + j]
                )
            )
            at += count * unit
        act_copies[masks[0]].start()
        og_copy.start()
        begun = {masks[0]}
        for j, (_, m, _) in enumerate(pieces):
            if m not in begun:
                act_copies[m].start()
                begun.add(m)
            stale_copies[j].start()
            if j == 0:
                tok_copy.start()
                trig_copy.start()
        tok_copy.wait()
        trig_copy.wait()
        real = (tok_ref[...] != 0).astype(BF16)
        weights = {}
        at, offset, last = 0, 0, -1
        for j, (i, m, (first, count)) in enumerate(pieces):
            offset = 0 if i != last else offset
            last = i
            if m not in weights:
                act_copies[m].wait()
                weights[m] = acts_buf[masks.index(m)].T * real
            if j == 0:
                og_copy.wait()
            part = weights[m][first * unit : (first + count) * unit]
            gradient = jnp.dot(part, og_buf[...], preferred_element_type=F32)
            stale_copies[j].wait()
            for b in range(0, count * unit, BLOCK):
                flag = trig_ref[0, (start[m] + first * unit + b) // BLOCK].astype(F32)
                old = stale_buf[at + b : at + b + BLOCK, :].astype(F32)
                outs[i][offset + b : offset + b + BLOCK, :] = (flag * (gradient[b : b + BLOCK] - old)).astype(BF16)
            at += count * unit
            offset += count * unit

    return pl.pallas_call(
        kernel,
        out_shape=tuple(jax.ShapeDtypeStruct((h, width), BF16) for h in heights),
        in_specs=[HBM] * 5,
        out_specs=tuple(VMEM for _ in messages),
        scratch_shapes=[
            pltpu.VMEM((len(masks), tokens, chunk), BF16),
            pltpu.VMEM((tokens, width), BF16),
            pltpu.VMEM((total, width), BF16),
            pltpu.VMEM(tok.shape, jnp.int32),
            pltpu.SMEM(trig.shape, jnp.int32),
            pltpu.SemaphoreType.DMA((2,)),
            pltpu.SemaphoreType.DMA((1 + len(masks) + len(pieces),)),
        ],
        cost_estimate=pl.CostEstimate(
            flops=2 * tokens * total * width, bytes_accessed=total * width * 4, transcendentals=0
        ),
        compiler_params=pltpu.CompilerParams(vmem_limit_bytes=limit),
    )(trig, tok, acts, og, stale)


def add_round(parts, rows):
    width = parts[0][0].shape[1]

    def kernel(*refs):
        out, lost = refs[-2:]
        energy = jnp.zeros((8, 128), F32)
        for r in range(0, rows, BLOCK):
            total = jnp.zeros((BLOCK, width), F32)
            for ref, (_, at) in zip(refs, parts):
                total = total + ref[at + r : at + r + BLOCK, :].astype(F32)
            rounded = total.astype(BF16)
            out[r : r + BLOCK, :] = rounded
            energy = energy + fold(total - rounded.astype(F32))
        lost[...] = energy

    return pl.pallas_call(
        kernel,
        out_shape=(jax.ShapeDtypeStruct((rows, width), BF16), jax.ShapeDtypeStruct((8, 128), F32)),
        in_specs=[VMEM] * len(parts),
        out_specs=(VMEM, VMEM),
        cost_estimate=pl.CostEstimate(flops=rows * width * 6, bytes_accessed=rows * width * 6, transcendentals=0),
        compiler_params=pltpu.CompilerParams(vmem_limit_bytes=12 * MIB),
    )(*[x for x, _ in parts])


def total_up(prev, groups, lost, trig, begun):
    arrays = {id(x): x for _, addends in groups for x, _ in addends}
    keys = list(arrays)
    flat = [x for group in lost for x in group]
    n_arrays, n_lost, n_begun = len(keys), len(flat), len(begun)
    lowest = min(first for (first, _), _ in groups)
    height = sum(rows for (_, rows), _ in groups)

    def kernel(trig_ref, prev_ref, *refs):
        lost_refs = list(refs[n_arrays : n_arrays + n_lost])
        before = refs[n_arrays + n_lost :][:n_begun]
        kept, sums = refs[n_arrays + n_lost + n_begun :]
        total = jnp.zeros((8, 128), F32)
        for (first, rows), addends in groups:
            for r in range(0, rows, BLOCK):
                a = prev_ref[0, first + r : first + r + BLOCK, :]
                for x, at in addends:
                    a = a + refs[keys.index(id(x))][at + r : at + r + BLOCK, :].astype(F32)
                kept[0, first - lowest + r : first - lowest + r + BLOCK, :] = a
                total = total + fold(a)
        row = lax.broadcasted_iota(jnp.int32, (8, 128), 0)
        if n_begun:
            stacked = before[0][...]
        else:
            stacked = jnp.where(row == 1, trig_ref[...].astype(F32), 0.0)
        stacked = stacked + jnp.where(row == 0, jnp.sum(total, axis=0, keepdims=True), 0.0)
        for i, group in enumerate(lost):
            tile = sum(lost_refs.pop(0)[...] for _ in group)
            stacked = jnp.where(row == 2 + i, jnp.sum(tile, axis=0, keepdims=True), stacked)
        if sums.shape == stacked.shape:
            sums[...] = stacked
        else:
            lane = lax.broadcasted_iota(jnp.int32, (8, 128), 1)
            values = jnp.sum(stacked, axis=1, keepdims=True)
            line = jnp.sum(jnp.where(row == lane, values, 0.0), axis=0, keepdims=True)
            sums[...] = jnp.broadcast_to(line[None], sums.shape)

    n = lax.axis_size("dp") * lax.axis_size("shard")
    ends = n_begun or height == prev.shape[1]
    return pl.pallas_call(
        kernel,
        out_shape=(
            jax.ShapeDtypeStruct((1, height, prev.shape[2]), F32),
            jax.ShapeDtypeStruct((n, 1, 128) if ends else (8, 128), F32),
        ),
        in_specs=[VMEM] * (2 + n_arrays + n_lost + n_begun),
        out_specs=(VMEM, VMEM),
        compiler_params=pltpu.CompilerParams(vmem_limit_bytes=12 * MIB),
    )(trig, prev, *arrays.values(), *flat, *begun)


def store(kept):
    shape = (1, sum(x.shape[1] for _, x in kept), kept[0][1].shape[2])

    def kernel(*refs):
        out, sem = refs[len(kept) :]
        copies = []
        for i, (first, x) in enumerate(kept):
            there = pl.ds(first, x.shape[1])
            copies.append(pltpu.make_async_copy(refs[i], out.at[:, there], sem.at[i]))
            copies[-1].start()
        for c in copies:
            c.wait()

    return pl.pallas_call(
        kernel,
        out_shape=jax.ShapeDtypeStruct(shape, F32),
        in_specs=[VMEM] * len(kept),
        out_specs=HBM,
        scratch_shapes=[pltpu.SemaphoreType.DMA((len(kept),))],
        cost_estimate=pl.CostEstimate(flops=0, bytes_accessed=1 << 24, transcendentals=0),
        compiler_params=pltpu.CompilerParams(vmem_limit_bytes=8 * MIB),
        name="store",
    )(*[x for _, x in kept])


def scale(kept, gathered):
    devices = gathered.shape[0]
    shape = (1, sum(x.shape[1] for _, x in kept), kept[0][1].shape[2])
    spans = []
    for i, (first, x) in enumerate(kept):
        step = PIECE if x.shape[1] % PIECE == 0 else BLOCK
        spans += [(i, r, first + r, step) for r in range(0, x.shape[1], step)]

    def kernel(*refs):
        all_ref, out, hits, bad, buf, sem = refs[len(kept) :]
        table = all_ref[:, 0, :]
        s = jnp.sum(table, axis=0, keepdims=True)
        lane = lax.broadcasted_iota(jnp.int32, (1, 128), 1)
        pick = lambda x, where: jnp.sum(jnp.where(where, x, 0.0), axis=1, keepdims=True)
        square_total = pick(s, lane == 0)
        limit = clip_ratio * jnp.sqrt(jnp.full((1, 1), HID * COLS, F32))
        factor = jnp.minimum(1.0, limit / jnp.sqrt(square_total + epsilon))
        copies = []
        for p, (i, r, first, step) in enumerate(spans):
            there = pl.ds(first, step)
            buf[0, first : first + step, :] = refs[i][0, r : r + step, :] * factor
            copies.append(pltpu.make_async_copy(buf.at[:, there], out.at[:, there], sem.at[p]))
            copies[-1].start()
        most = jnp.max(table, axis=0, keepdims=True)
        hits[...] = pick(s, lane == 1)
        roundings = (lane >= 2) & (lane < 2 + STAGES)
        room = (ROUNDING * ROUNDING / STAGES) * square_total
        over = (pick(s, roundings) > room) | (devices * pick(most, roundings) > 2.0 * room)
        bad[...] = over.astype(jnp.int32)
        for c in copies:
            c.wait()

    one = lambda t: jax.ShapeDtypeStruct((1, 1), t)
    return pl.pallas_call(
        kernel,
        out_shape=(jax.ShapeDtypeStruct(shape, F32), one(F32), one(jnp.int32)),
        in_specs=[VMEM] * (len(kept) + 1),
        out_specs=(HBM, VMEM, VMEM),
        scratch_shapes=[pltpu.VMEM(shape, F32), pltpu.SemaphoreType.DMA((len(spans),))],
        compiler_params=pltpu.CompilerParams(vmem_limit_bytes=8 * MIB),
        name="scale",
    )(*[x for _, x in kept], gathered)


def local(*args):
    return step(*args)


def step(hidden_acts, out_grad, token_ids, trigger, stale, aggregate_prev):
    n = lax.axis_size("dp")
    chunk = aggregate_prev.shape[1]
    unit = chunk // 16
    args = (trigger, token_ids, hidden_acts, out_grad, stale)

    def swap(x, mask):
        return lax.ppermute(x, "dp", [(i, i ^ mask) for i in range(n)])

    outgoing = [[(m ^ bit, rows) for m, rows in parts] for _, bit, parts in RAW]
    made = list(deltas(*args, outgoing[:FIRST], chunk, 60 * 1024 * 1024))
    rest = deltas(*args, outgoing[FIRST:] + [[key] for key in OWN_EARLY], chunk, 16 * MIB)
    made += rest[: len(RAW) - FIRST]
    got = {label: swap(x, bit) for (label, bit, _), x in zip(RAW, made)}
    own = dict(zip(OWN_EARLY, rest[len(RAW) - FIRST :]))
    own.update(zip(OWN_LATE, deltas(*args, [[key] for key in OWN_LATE], chunk, 16 * MIB)))
    lost = [[] for _ in range(STAGES)]
    for label, bit, mine, others, group in SUMS:
        parts = [(own[mine], 0)] + [(got[name], k * mine[1][1] * unit) for name, k in others]
        total, energy = add_round(parts, mine[1][1] * unit)
        lost[group].append(energy)
        got[label] = swap(total, bit)

    def addends(table):
        pieces = []
        for (first, count), mine, others in table:
            terms = [(own[mine], 0)] + [(got[name], k * count * unit) for name, k in others]
            pieces.append(((first * unit, count * unit), terms))
        return pieces

    kept, sums = total_up(aggregate_prev, addends(FINAL), lost, trigger, ())
    kept_last, sums = total_up(aggregate_prev, addends(LAST), [], trigger, (sums,))
    everyone = lax.all_to_all(sums, ("dp", "shard"), 0, 0, tiled=True)
    kept = [(0, kept_last), (A0[1] * unit, kept)]
    agg = store(kept)
    update, hits, bad = scale(kept, everyone)

    def again(state):
        mine = deltas(*args, [[(m, (0, 16))] for m in range(n)], chunk, 24 * MIB)
        came = [mine[0]] + [lax.ppermute(mine[m], "dp", [(i, i ^ m) for i in range(n)]) for m in range(1, n)]
        whole = [((0, chunk), [(x, 0) for x in came])]
        new_kept, new_sums = total_up(aggregate_prev, whole, [], trigger, ())
        new_update, _, _ = scale([(0, new_kept)], lax.all_to_all(new_sums, ("dp", "shard"), 0, 0, tiled=True))
        return jnp.zeros((), jnp.int32), new_kept, new_update

    _, agg, update = lax.while_loop(lambda state: state[0] > 0, again, (bad[0, 0], agg, update))
    return agg, update, hits[0, 0]


def exact(hidden_acts, out_grad, token_ids, trigger, stale, aggregate_prev):
    masked = out_grad[0] * (token_ids[0] != 0).astype(BF16)[:, None]
    row_flags = jnp.repeat(trigger[0], BLOCK).astype(F32)[:, None]
    triggered = lax.psum(jnp.sum(trigger.astype(F32)), ("dp", "shard"))
    gradient = lax.dot_general(hidden_acts[0], masked, (((0,), (0,)), ((), ())), preferred_element_type=F32)
    delta = (row_flags * (gradient - stale[0].astype(F32))).astype(BF16)
    delta = delta.reshape(lax.axis_size("dp"), aggregate_prev.shape[1], stale.shape[2])
    received = lax.all_to_all(delta, "dp", split_axis=0, concat_axis=0, tiled=True)
    aggregate = aggregate_prev[0] + jnp.sum(received, axis=0, dtype=F32)
    square_total = lax.psum(jnp.sum(aggregate * aggregate), ("dp", "shard"))
    limit = clip_ratio * jnp.sqrt(jnp.asarray(HID * COLS, F32))
    factor = jnp.minimum(1.0, limit / jnp.sqrt(square_total + epsilon))
    return aggregate[None], (aggregate * factor)[None], triggered


def solution(mesh):
    staged = mesh.shape["dp"] == 8
    return jax.shard_map(
        local if staged else exact,
        mesh=mesh,
        in_specs=(
            P("dp", None, "shard"),
            P("dp", None, None),
            P("dp", None),
            P("dp", "shard"),
            P("dp", "shard", None),
            P("shard", "dp", None),
        ),
        out_specs=(P("shard", "dp", None), P("shard", "dp", None), P()),
        check_vma=False,
    )
```

```python
import jax
import jax.numpy as jnp
from jax import lax
from jax.experimental import pallas as pl
from jax.experimental.pallas import tpu as pltpu
from jax.sharding import PartitionSpec as P

COLS = 1024
HID = 8192
BLOCK = 16
clip_ratio = 0.25
epsilon = 1e-06
MIB = 1 << 20
PIECE = 64
STAGES = 3
ROUNDING = 4.8e-4
F32, BF16 = jnp.float32, jnp.bfloat16
VMEM = pl.BlockSpec(memory_space=pltpu.VMEM)
SMEM = pl.BlockSpec(memory_space=pltpu.SMEM)
HBM = pl.BlockSpec(memory_space=pltpu.HBM)

A0, A1, B = (0, 6), (6, 6), (12, 4)
RAW = (
    ("y6a", 1, ((6, A0),)),
    ("zb0", 2, ((5, B), (4, B))),
    ("y4a", 1, ((4, A0),)),
    ("y6b", 1, ((6, A1),)),
    ("zb1", 2, ((1, B), (0, B))),
    ("y4b", 1, ((4, A1),)),
    ("y2a", 1, ((2, A0),)),
    ("y2b", 1, ((2, A1),)),
    ("y0b", 1, ((0, A1),)),
    ("y0a", 1, ((0, A0),)),
)
FIRST = 3
OWN_EARLY = ((6, A0), (5, B), (4, A0), (6, A1))
OWN_LATE = ((4, B), (4, A1), (1, B), (2, A0), (2, A1), (0, A0), (0, A1), (0, B))
SUMS = (
    ("near0", 2, (6, A0), (("y6a", 0),), 0),
    ("pairb5", 1, (5, B), (("zb0", 0),), 0),
    ("quad0", 4, (4, A0), (("y4a", 0), ("near0", 0)), 1),
    ("near1", 2, (6, A1), (("y6b", 0),), 0),
    ("pairb1", 1, (1, B), (("zb1", 0),), 2),
    ("quadb", 4, (4, B), (("zb0", 1), ("pairb5", 0)), 1),
    ("quad1", 4, (4, A1), (("y4b", 0), ("near1", 0)), 1),
    ("last0", 2, (2, A0), (("y2a", 0),), 2),
    ("last1", 2, (2, A1), (("y2b", 0),), 2),
)
FINAL = (
    (B, (0, B), (("zb1", 1), ("pairb1", 0), ("quadb", 0))),
    (A1, (0, A1), (("y0b", 0), ("last1", 0), ("quad1", 0))),
)
LAST = ((A0, (0, A0), (("y0a", 0), ("last0", 0), ("quad0", 0))),)


def fold(x):
    sq = x * x
    total = jnp.zeros((8, 128), F32)
    for c in range(0, x.shape[1], 128):
        for r in range(0, x.shape[0], 8):
            total = total + sq[r : r + 8, c : c + 128]
    return total


def plan(messages, chunk):
    unit = chunk // 16
    pieces, heights = [], []
    for i, message in enumerate(messages):
        at = 0
        for mask, (first, count) in message:
            pieces.append((i, at, mask, first * unit, count * unit))
            at += count * unit
        heights.append(at)
    return pieces, list(dict.fromkeys(p[2] for p in pieces)), heights


def piece_rows(weights, og, old, trig_ref, block, out):
    gradient = jnp.dot(weights, og, preferred_element_type=F32)
    for b in range(0, gradient.shape[0], BLOCK):
        flag = trig_ref[0, block + b // BLOCK].astype(F32)
        out[b : b + BLOCK, :] = (flag * (gradient[b : b + BLOCK] - old(b).astype(F32))).astype(BF16)


def deltas_first(trig, tok, acts, og, stale, messages, chunk):
    tokens, width = og.shape[1], og.shape[2]
    pieces, masks, heights = plan(messages, chunk)
    total, n_out = sum(heights), len(messages)

    def kernel(trig_hbm, tok_hbm, acts_hbm, og_hbm, stale_hbm, *refs):
        outs = refs[:n_out]
        acts_buf, og_buf, stale_buf, tok_ref, trig_ref, sem = refs[n_out : n_out + 6]
        me = lax.axis_index("dp")
        start = {m: pl.multiple_of((me ^ m) * chunk, chunk) for m in masks}
        sems = iter(range(3 + len(masks) + len(pieces)))
        begin = lambda source, target: pltpu.make_async_copy(source, target, sem.at[next(sems)])
        acts_of = lambda j: begin(acts_hbm.at[0, :, pl.ds(start[masks[j]], chunk)], acts_buf.at[j])
        first_acts, og_copy = acts_of(0), begin(og_hbm.at[0], og_buf)
        tok_copy, trig_copy = begin(tok_hbm, tok_ref), begin(trig_hbm, trig_ref)
        stale_copies, at = [], 0
        for _, _, m, first, rows in pieces:
            source = stale_hbm.at[0, pl.ds(pl.multiple_of(start[m] + first, BLOCK), rows), :]
            stale_copies.append(begin(source, stale_buf.at[pl.ds(at, rows), :]))
            at += rows
        act_copies = [first_acts] + [acts_of(j) for j in range(1, len(masks))]
        for copy in [first_acts, og_copy, stale_copies[0], tok_copy, trig_copy] + act_copies[1:] + stale_copies[1:]:
            copy.start()
        tok_copy.wait()
        trig_copy.wait()
        real = (tok_ref[...] != 0).astype(BF16)
        weights, at = {}, 0
        for j, (i, offset, m, first, rows) in enumerate(pieces):
            if m not in weights:
                act_copies[masks.index(m)].wait()
                weights[m] = acts_buf[masks.index(m)].T * real
            if j == 0:
                og_copy.wait()
            stale_copies[j].wait()
            old = lambda b, at=at: stale_buf[at + b : at + b + BLOCK, :]
            block = (start[m] + first) // BLOCK
            piece_rows(
                weights[m][first : first + rows], og_buf[...], old, trig_ref, block, outs[i].at[pl.ds(offset, rows), :]
            )
            at += rows

    return pl.pallas_call(
        kernel,
        out_shape=tuple(jax.ShapeDtypeStruct((h, width), BF16) for h in heights),
        in_specs=[HBM] * 5,
        out_specs=tuple(VMEM for _ in messages),
        scratch_shapes=[
            pltpu.VMEM((len(masks), tokens, chunk), BF16),
            pltpu.VMEM((tokens, width), BF16),
            pltpu.VMEM((total, width), BF16),
            pltpu.VMEM(tok.shape, jnp.int32),
            pltpu.SMEM(trig.shape, jnp.int32),
            pltpu.SemaphoreType.DMA((4 + len(masks) + len(pieces),)),
        ],
        cost_estimate=pl.CostEstimate(
            flops=2 * tokens * total * width, bytes_accessed=total * width * 4, transcendentals=0
        ),
        compiler_params=pltpu.CompilerParams(vmem_limit_bytes=16 * MIB),
    )(trig, tok, acts, og, stale)


def deltas(trig, tok, acts, og, stale, messages, chunk):
    tokens, width = og.shape[1], og.shape[2]
    pieces, masks, heights = plan(messages, chunk)

    def kernel(trig_hbm, tok_ref, acts_ref, og_ref, stale_ref, *refs):
        outs, (trig_ref, sem) = refs[:-2], refs[-2:]
        trig_copy = pltpu.make_async_copy(trig_hbm, trig_ref, sem.at[0])
        trig_copy.start()
        me = lax.axis_index("dp")
        start = {m: pl.multiple_of((me ^ m) * chunk, chunk) for m in masks}
        real = (tok_ref[...] != 0).astype(BF16)
        weights = {}
        for j, (i, offset, m, first, rows) in enumerate(pieces):
            if m not in weights:
                weights[m] = acts_ref[0, :, pl.ds(start[m], chunk)].T * real
            if j == 0:
                trig_copy.wait()
            old = lambda b, m=m, first=first: stale_ref[0, pl.ds(pl.multiple_of(start[m] + first + b, BLOCK), BLOCK), :]
            block = (start[m] + first) // BLOCK
            piece_rows(
                weights[m][first : first + rows], og_ref[0], old, trig_ref, block, outs[i].at[pl.ds(offset, rows), :]
            )

    total = sum(heights)
    return pl.pallas_call(
        kernel,
        out_shape=tuple(jax.ShapeDtypeStruct((h, width), BF16) for h in heights),
        in_specs=[HBM] + [VMEM] * 4,
        out_specs=tuple(VMEM for _ in messages),
        scratch_shapes=[pltpu.SMEM(trig.shape, jnp.int32), pltpu.SemaphoreType.DMA((1,))],
        cost_estimate=pl.CostEstimate(
            flops=2 * tokens * total * width, bytes_accessed=total * width * 4, transcendentals=0
        ),
        compiler_params=pltpu.CompilerParams(vmem_limit_bytes=16 * MIB),
    )(trig, tok, acts, og, stale)


def add_round(parts, rows):
    width = parts[0][0].shape[1]

    def kernel(*refs):
        out, lost = refs[-2:]
        energy = jnp.zeros((8, 128), F32)
        for r in range(0, rows, BLOCK):
            total = jnp.zeros((BLOCK, width), F32)
            for ref, (_, at) in zip(refs, parts):
                total = total + ref[at + r : at + r + BLOCK, :].astype(F32)
            rounded = total.astype(BF16)
            out[r : r + BLOCK, :] = rounded
            energy = energy + fold(total - rounded.astype(F32))
        lost[...] = energy

    return pl.pallas_call(
        kernel,
        out_shape=(jax.ShapeDtypeStruct((rows, width), BF16), jax.ShapeDtypeStruct((8, 128), F32)),
        in_specs=[VMEM] * len(parts),
        out_specs=(VMEM, VMEM),
        cost_estimate=pl.CostEstimate(flops=rows * width * 6, bytes_accessed=rows * width * 6, transcendentals=0),
        compiler_params=pltpu.CompilerParams(vmem_limit_bytes=12 * MIB),
    )(*[x for x, _ in parts])


def total_up(prev, groups, lost, trig, begun):
    arrays = {id(x): x for _, addends in groups for x, _ in addends}
    keys = list(arrays)
    flat = [x for group in lost for x in group]
    n_arrays, n_lost, n_begun = len(keys), len(flat), len(begun)
    lowest = min(first for (first, _), _ in groups)
    height = sum(rows for (_, rows), _ in groups)

    def kernel(trig_ref, prev_ref, *refs):
        lost_refs = list(refs[n_arrays : n_arrays + n_lost])
        before = refs[n_arrays + n_lost :][:n_begun]
        kept, sums = refs[n_arrays + n_lost + n_begun :]
        total = jnp.zeros((8, 128), F32)
        for (first, rows), addends in groups:
            for r in range(0, rows, BLOCK):
                a = prev_ref[0, first + r : first + r + BLOCK, :]
                for x, at in addends:
                    a = a + refs[keys.index(id(x))][at + r : at + r + BLOCK, :].astype(F32)
                kept[0, first - lowest + r : first - lowest + r + BLOCK, :] = a
                total = total + fold(a)
        row = lax.broadcasted_iota(jnp.int32, (8, 128), 0)
        if n_begun:
            stacked = before[0][...]
        else:
            stacked = jnp.where(row == 1, trig_ref[...].astype(F32), 0.0)
        stacked = stacked + jnp.where(row == 0, jnp.sum(total, axis=0, keepdims=True), 0.0)
        for i, group in enumerate(lost):
            tile = sum(lost_refs.pop(0)[...] for _ in group)
            stacked = jnp.where(row == 2 + i, jnp.sum(tile, axis=0, keepdims=True), stacked)
        if sums.shape == stacked.shape:
            sums[...] = stacked
        else:
            lane = lax.broadcasted_iota(jnp.int32, (8, 128), 1)
            values = jnp.sum(stacked, axis=1, keepdims=True)
            line = jnp.sum(jnp.where(row == lane, values, 0.0), axis=0, keepdims=True)
            sums[...] = jnp.broadcast_to(line[None], sums.shape)

    n = lax.axis_size("dp") * lax.axis_size("shard")
    ends = n_begun or height == prev.shape[1]
    return pl.pallas_call(
        kernel,
        out_shape=(
            jax.ShapeDtypeStruct((1, height, prev.shape[2]), F32),
            jax.ShapeDtypeStruct((n, 1, 128) if ends else (8, 128), F32),
        ),
        in_specs=[VMEM] * (2 + n_arrays + n_lost + n_begun),
        out_specs=(VMEM, VMEM),
        compiler_params=pltpu.CompilerParams(vmem_limit_bytes=12 * MIB),
    )(trig, prev, *arrays.values(), *flat, *begun)


def store(kept):
    shape = (1, sum(x.shape[1] for _, x in kept), kept[0][1].shape[2])

    def kernel(*refs):
        out, sem = refs[len(kept) :]
        copies = []
        for i, (first, x) in enumerate(kept):
            there = pl.ds(first, x.shape[1])
            copies.append(pltpu.make_async_copy(refs[i], out.at[:, there], sem.at[i]))
            copies[-1].start()
        for c in copies:
            c.wait()

    return pl.pallas_call(
        kernel,
        out_shape=jax.ShapeDtypeStruct(shape, F32),
        in_specs=[VMEM] * len(kept),
        out_specs=HBM,
        scratch_shapes=[pltpu.SemaphoreType.DMA((len(kept),))],
        cost_estimate=pl.CostEstimate(flops=0, bytes_accessed=1 << 24, transcendentals=0),
        compiler_params=pltpu.CompilerParams(vmem_limit_bytes=8 * MIB),
        name="store",
    )(*[x for _, x in kept])


def scale(kept, gathered):
    devices = gathered.shape[0]
    shape = (1, sum(x.shape[1] for _, x in kept), kept[0][1].shape[2])
    spans = []
    for i, (first, x) in enumerate(kept):
        step = PIECE if x.shape[1] % PIECE == 0 else BLOCK
        spans += [(i, r, first + r, step) for r in range(0, x.shape[1], step)]

    def kernel(*refs):
        all_ref, out, hits_out, bad_out, buf, hits, bad, sem = refs[len(kept) :]
        table = all_ref[:, 0, :]
        s = jnp.sum(table, axis=0, keepdims=True)
        lane = lax.broadcasted_iota(jnp.int32, (1, 128), 1)
        pick = lambda x, where: jnp.sum(jnp.where(where, x, 0.0), axis=1, keepdims=True)
        square_total = pick(s, lane == 0)
        limit = clip_ratio * jnp.sqrt(jnp.full((1, 1), HID * COLS, F32))
        factor = jnp.minimum(1.0, limit / jnp.sqrt(square_total + epsilon))
        copies = []
        for p, (i, r, first, step) in enumerate(spans):
            there = pl.ds(first, step)
            buf[0, first : first + step, :] = refs[i][0, r : r + step, :] * factor
            copies.append(pltpu.make_async_copy(buf.at[:, there], out.at[:, there], sem.at[p]))
            copies[-1].start()
        most = jnp.max(table, axis=0, keepdims=True)
        n = len(spans)
        hits[...] = pick(s, lane == 1)
        roundings = (lane >= 2) & (lane < 2 + STAGES)
        room = (ROUNDING * ROUNDING / STAGES) * square_total
        over = (pick(s, roundings) > room) | (devices * pick(most, roundings) > 2.0 * room)
        bad[...] = over.astype(jnp.int32)
        copies.append(pltpu.make_async_copy(hits, hits_out, sem.at[n]))
        copies.append(pltpu.make_async_copy(bad, bad_out, sem.at[n + 1]))
        copies[n].start()
        copies[n + 1].start()
        for c in copies:
            c.wait()

    one = lambda t: jax.ShapeDtypeStruct((1, 1), t)
    return pl.pallas_call(
        kernel,
        out_shape=(jax.ShapeDtypeStruct(shape, F32), one(F32), one(jnp.int32)),
        in_specs=[VMEM] * (len(kept) + 1),
        out_specs=(HBM, HBM, HBM),
        scratch_shapes=[
            pltpu.VMEM(shape, F32),
            pltpu.VMEM((1, 1), F32),
            pltpu.VMEM((1, 1), jnp.int32),
            pltpu.SemaphoreType.DMA((len(spans) + 2,)),
        ],
        compiler_params=pltpu.CompilerParams(vmem_limit_bytes=8 * MIB),
        name="scale",
    )(*[x for _, x in kept], gathered)


def local(*args):
    return step(*args)


def step(hidden_acts, out_grad, token_ids, trigger, stale, aggregate_prev):
    n = lax.axis_size("dp")
    chunk = aggregate_prev.shape[1]
    unit = chunk // 16
    args = (trigger, token_ids, hidden_acts, out_grad, stale)

    def swap(x, mask):
        return lax.ppermute(x, "dp", [(i, i ^ mask) for i in range(n)])

    outgoing = [[(m ^ bit, rows) for m, rows in parts] for _, bit, parts in RAW]
    made = list(deltas_first(*args, outgoing[:FIRST], chunk))
    rest = deltas(*args, outgoing[FIRST:] + [[key] for key in OWN_EARLY], chunk)
    made += rest[: len(RAW) - FIRST]
    got = {label: swap(x, bit) for (label, bit, _), x in zip(RAW, made)}
    own = dict(zip(OWN_EARLY, rest[len(RAW) - FIRST :]))
    own.update(zip(OWN_LATE, deltas(*args, [[key] for key in OWN_LATE], chunk)))
    lost = [[] for _ in range(STAGES)]
    for label, bit, mine, others, group in SUMS:
        parts = [(own[mine], 0)] + [(got[name], k * mine[1][1] * unit) for name, k in others]
        total, energy = add_round(parts, mine[1][1] * unit)
        lost[group].append(energy)
        got[label] = swap(total, bit)

    def addends(table):
        pieces = []
        for (first, count), mine, others in table:
            terms = [(own[mine], 0)] + [(got[name], k * count * unit) for name, k in others]
            pieces.append(((first * unit, count * unit), terms))
        return pieces

    kept, sums = total_up(aggregate_prev, addends(FINAL), lost, trigger, ())
    kept_last, sums = total_up(aggregate_prev, addends(LAST), [], trigger, (sums,))
    everyone = lax.all_to_all(sums, ("dp", "shard"), 0, 0, tiled=True)
    kept = [(0, kept_last), (A0[1] * unit, kept)]
    agg = store(kept)
    update, hits, bad = scale(kept, everyone)

    def again(state):
        mine = deltas(*args, [[(m, (0, 16))] for m in range(n)], chunk)
        came = [mine[0]] + [lax.ppermute(mine[m], "dp", [(i, i ^ m) for i in range(n)]) for m in range(1, n)]
        whole = [((0, chunk), [(x, 0) for x in came])]
        new_kept, new_sums = total_up(aggregate_prev, whole, [], trigger, ())
        new_update, _, _ = scale([(0, new_kept)], lax.all_to_all(new_sums, ("dp", "shard"), 0, 0, tiled=True))
        return jnp.zeros((), jnp.int32), new_kept, new_update

    _, agg, update = lax.while_loop(lambda state: state[0] > 0, again, (bad[0, 0], agg, update))
    return agg, update, hits[0, 0]


def exact(hidden_acts, out_grad, token_ids, trigger, stale, aggregate_prev):
    masked = out_grad[0] * (token_ids[0] != 0).astype(BF16)[:, None]
    row_flags = jnp.repeat(trigger[0], BLOCK).astype(F32)[:, None]
    triggered = lax.psum(jnp.sum(trigger.astype(F32)), ("dp", "shard"))
    gradient = lax.dot_general(hidden_acts[0], masked, (((0,), (0,)), ((), ())), preferred_element_type=F32)
    delta = (row_flags * (gradient - stale[0].astype(F32))).astype(BF16)
    delta = delta.reshape(lax.axis_size("dp"), aggregate_prev.shape[1], stale.shape[2])
    received = lax.all_to_all(delta, "dp", split_axis=0, concat_axis=0, tiled=True)
    aggregate = aggregate_prev[0] + jnp.sum(received, axis=0, dtype=F32)
    square_total = lax.psum(jnp.sum(aggregate * aggregate), ("dp", "shard"))
    limit = clip_ratio * jnp.sqrt(jnp.asarray(HID * COLS, F32))
    factor = jnp.minimum(1.0, limit / jnp.sqrt(square_total + epsilon))
    return aggregate[None], (aggregate * factor)[None], triggered


def solution(mesh):
    staged = mesh.shape["dp"] == 8
    return jax.shard_map(
        local if staged else exact,
        mesh=mesh,
        in_specs=(
            P("dp", None, "shard"),
            P("dp", None, None),
            P("dp", None),
            P("dp", "shard"),
            P("dp", "shard", None),
            P("shard", "dp", None),
        ),
        out_specs=(P("shard", "dp", None), P("shard", "dp", None), P()),
        check_vma=False,
    )
```

```python
import jax
import jax.numpy as jnp
from jax import lax
from jax.experimental import pallas as pl
from jax.experimental.pallas import tpu as pltpu
from jax.sharding import PartitionSpec as P

COLS = 1024
HID = 8192
BLOCK = 16
clip_ratio = 0.25
epsilon = 1e-06
MIB = 1 << 20
PIECE = 64
STAGES = 3
KINDS = 6
ROUNDING = 4.8e-4
F32, BF16 = jnp.float32, jnp.bfloat16
VMEM = pl.BlockSpec(memory_space=pltpu.VMEM)
SMEM = pl.BlockSpec(memory_space=pltpu.SMEM)
HBM = pl.BlockSpec(memory_space=pltpu.HBM)

A0, A1, B = (0, 6), (6, 6), (12, 4)
RAW = (
    ("y6a", 1, ((6, A0),)),
    ("zb0", 2, ((5, B), (4, B))),
    ("y4a", 1, ((4, A0),)),
    ("y6b", 1, ((6, A1),)),
    ("zb1", 2, ((1, B), (0, B))),
    ("y4b", 1, ((4, A1),)),
    ("y2a", 1, ((2, A0),)),
    ("y2b", 1, ((2, A1),)),
    ("y0b", 1, ((0, A1),)),
    ("y0a", 1, ((0, A0),)),
)
FIRST = 2
OWN_EARLY = ((6, A0), (5, B), (4, A0), (6, A1))
OWN_LATE = ((4, B), (4, A1), (1, B), (2, A0), (2, A1), (0, A0), (0, A1), (0, B))
SUMS = (
    ("near0", 2, (6, A0), (("y6a", 0),), 0),
    ("pairb5", 1, (5, B), (("zb0", 0),), 3),
    ("quad0", 4, (4, A0), (("y4a", 0), ("near0", 0)), 1),
    ("near1", 2, (6, A1), (("y6b", 0),), 0),
    ("pairb1", 1, (1, B), (("zb1", 0),), 5),
    ("quadb", 4, (4, B), (("zb0", 1), ("pairb5", 0)), 4),
    ("quad1", 4, (4, A1), (("y4b", 0), ("near1", 0)), 1),
    ("last0", 2, (2, A0), (("y2a", 0),), 2),
    ("last1", 2, (2, A1), (("y2b", 0),), 2),
)
FINAL = (
    (B, (0, B), (("zb1", 1), ("pairb1", 0), ("quadb", 0))),
    (A1, (0, A1), (("y0b", 0), ("last1", 0), ("quad1", 0))),
)
LAST = ((A0, (0, A0), (("y0a", 0), ("last0", 0), ("quad0", 0))),)


def fold(x):
    sq = x * x
    total = jnp.zeros((8, 128), F32)
    for c in range(0, x.shape[1], 128):
        for r in range(0, x.shape[0], 8):
            total = total + sq[r : r + 8, c : c + 128]
    return total


def plan(messages, chunk):
    unit = chunk // 16
    pieces, heights = [], []
    for i, message in enumerate(messages):
        at = 0
        for mask, (first, count) in message:
            pieces.append((i, at, mask, first * unit, count * unit))
            at += count * unit
        heights.append(at)
    return pieces, list(dict.fromkeys(p[2] for p in pieces)), heights


def piece_rows(weights, og, old, trig_ref, block, out):
    gradient = jnp.dot(weights, og, preferred_element_type=F32)
    for b in range(0, gradient.shape[0], BLOCK):
        flag = trig_ref[0, block + b // BLOCK].astype(F32)
        out[b : b + BLOCK, :] = (flag * (gradient[b : b + BLOCK] - old(b).astype(F32))).astype(BF16)


def deltas_first(trig, tok, acts, og, stale, messages, chunk):
    tokens, width = og.shape[1], og.shape[2]
    pieces, masks, heights = plan(messages, chunk)
    total, n_out = sum(heights), len(messages)

    def kernel(trig_hbm, tok_hbm, acts_hbm, og_hbm, stale_hbm, *refs):
        outs = refs[:n_out]
        acts_buf, og_buf, stale_buf, tok_ref, trig_ref, sem = refs[n_out : n_out + 6]
        me = lax.axis_index("dp")
        start = {m: pl.multiple_of((me ^ m) * chunk, chunk) for m in masks}
        sems = iter(range(3 + len(masks) + len(pieces)))
        begin = lambda source, target: pltpu.make_async_copy(source, target, sem.at[next(sems)])
        acts_of = lambda j: begin(acts_hbm.at[0, :, pl.ds(start[masks[j]], chunk)], acts_buf.at[j])
        first_acts, og_copy = acts_of(0), begin(og_hbm.at[0], og_buf)
        tok_copy, trig_copy = begin(tok_hbm, tok_ref), begin(trig_hbm, trig_ref)
        stale_copies, at = [], 0
        for _, _, m, first, rows in pieces:
            source = stale_hbm.at[0, pl.ds(pl.multiple_of(start[m] + first, BLOCK), rows), :]
            stale_copies.append(begin(source, stale_buf.at[pl.ds(at, rows), :]))
            at += rows
        act_copies = [first_acts] + [acts_of(j) for j in range(1, len(masks))]
        for copy in [first_acts, og_copy, stale_copies[0], tok_copy, trig_copy] + act_copies[1:] + stale_copies[1:]:
            copy.start()
        tok_copy.wait()
        trig_copy.wait()
        real = (tok_ref[...] != 0).astype(BF16)
        weights, at = {}, 0
        for j, (i, offset, m, first, rows) in enumerate(pieces):
            if m not in weights:
                act_copies[masks.index(m)].wait()
                weights[m] = acts_buf[masks.index(m)].T * real
            if j == 0:
                og_copy.wait()
            stale_copies[j].wait()
            old = lambda b, at=at: stale_buf[at + b : at + b + BLOCK, :]
            block = (start[m] + first) // BLOCK
            piece_rows(
                weights[m][first : first + rows], og_buf[...], old, trig_ref, block, outs[i].at[pl.ds(offset, rows), :]
            )
            at += rows

    return pl.pallas_call(
        kernel,
        out_shape=tuple(jax.ShapeDtypeStruct((h, width), BF16) for h in heights),
        in_specs=[HBM] * 5,
        out_specs=tuple(VMEM for _ in messages),
        scratch_shapes=[
            pltpu.VMEM((len(masks), tokens, chunk), BF16),
            pltpu.VMEM((tokens, width), BF16),
            pltpu.VMEM((total, width), BF16),
            pltpu.VMEM(tok.shape, jnp.int32),
            pltpu.SMEM(trig.shape, jnp.int32),
            pltpu.SemaphoreType.DMA((4 + len(masks) + len(pieces),)),
        ],
        cost_estimate=pl.CostEstimate(
            flops=2 * tokens * total * width, bytes_accessed=total * width * 4, transcendentals=0
        ),
        compiler_params=pltpu.CompilerParams(vmem_limit_bytes=16 * MIB),
    )(trig, tok, acts, og, stale)


def deltas(trig, tok, acts, og, stale, messages, chunk):
    tokens, width = og.shape[1], og.shape[2]
    pieces, masks, heights = plan(messages, chunk)

    def kernel(trig_hbm, tok_ref, acts_ref, og_ref, stale_ref, *refs):
        outs, (trig_ref, sem) = refs[:-2], refs[-2:]
        trig_copy = pltpu.make_async_copy(trig_hbm, trig_ref, sem.at[0])
        trig_copy.start()
        me = lax.axis_index("dp")
        start = {m: pl.multiple_of((me ^ m) * chunk, chunk) for m in masks}
        real = (tok_ref[...] != 0).astype(BF16)
        weights = {}
        for j, (i, offset, m, first, rows) in enumerate(pieces):
            if m not in weights:
                weights[m] = acts_ref[0, :, pl.ds(start[m], chunk)].T * real
            if j == 0:
                trig_copy.wait()
            old = lambda b, m=m, first=first: stale_ref[0, pl.ds(pl.multiple_of(start[m] + first + b, BLOCK), BLOCK), :]
            block = (start[m] + first) // BLOCK
            piece_rows(
                weights[m][first : first + rows], og_ref[0], old, trig_ref, block, outs[i].at[pl.ds(offset, rows), :]
            )

    total = sum(heights)
    return pl.pallas_call(
        kernel,
        out_shape=tuple(jax.ShapeDtypeStruct((h, width), BF16) for h in heights),
        in_specs=[HBM] + [VMEM] * 4,
        out_specs=tuple(VMEM for _ in messages),
        scratch_shapes=[pltpu.SMEM(trig.shape, jnp.int32), pltpu.SemaphoreType.DMA((1,))],
        cost_estimate=pl.CostEstimate(
            flops=2 * tokens * total * width, bytes_accessed=total * width * 4, transcendentals=0
        ),
        compiler_params=pltpu.CompilerParams(vmem_limit_bytes=16 * MIB),
    )(trig, tok, acts, og, stale)


def add_round(parts, rows):
    width = parts[0][0].shape[1]

    def kernel(*refs):
        out, lost = refs[-2:]
        energy = jnp.zeros((8, 128), F32)
        for r in range(0, rows, BLOCK):
            total = jnp.zeros((BLOCK, width), F32)
            for ref, (_, at) in zip(refs, parts):
                total = total + ref[at + r : at + r + BLOCK, :].astype(F32)
            rounded = total.astype(BF16)
            out[r : r + BLOCK, :] = rounded
            energy = energy + fold(total - rounded.astype(F32))
        lost[...] = energy

    return pl.pallas_call(
        kernel,
        out_shape=(jax.ShapeDtypeStruct((rows, width), BF16), jax.ShapeDtypeStruct((8, 128), F32)),
        in_specs=[VMEM] * len(parts),
        out_specs=(VMEM, VMEM),
        cost_estimate=pl.CostEstimate(flops=rows * width * 6, bytes_accessed=rows * width * 6, transcendentals=0),
        compiler_params=pltpu.CompilerParams(vmem_limit_bytes=12 * MIB),
    )(*[x for x, _ in parts])


def total_up(prev, groups, lost, trig, begun):
    arrays = {id(x): x for _, addends in groups for x, _ in addends}
    keys = list(arrays)
    flat = [x for group in lost for x in group]
    n_arrays, n_lost, n_begun = len(keys), len(flat), len(begun)
    lowest = min(first for (first, _), _ in groups)
    height = sum(rows for (_, rows), _ in groups)

    def kernel(trig_ref, prev_ref, *refs):
        lost_refs = list(refs[n_arrays : n_arrays + n_lost])
        before = refs[n_arrays + n_lost :][:n_begun]
        kept, sums = refs[n_arrays + n_lost + n_begun :]
        total = jnp.zeros((8, 128), F32)
        for (first, rows), addends in groups:
            for r in range(0, rows, BLOCK):
                a = prev_ref[0, first + r : first + r + BLOCK, :]
                for x, at in addends:
                    a = a + refs[keys.index(id(x))][at + r : at + r + BLOCK, :].astype(F32)
                kept[0, first - lowest + r : first - lowest + r + BLOCK, :] = a
                total = total + fold(a)
        row = lax.broadcasted_iota(jnp.int32, (8, 128), 0)
        if n_begun:
            stacked = before[0][...]
        else:
            stacked = jnp.where(row == 1, trig_ref[...].astype(F32), 0.0)
        stacked = stacked + jnp.where(row == 0, jnp.sum(total, axis=0, keepdims=True), 0.0)
        for i, group in enumerate(lost):
            tile = sum(lost_refs.pop(0)[...] for _ in group)
            stacked = jnp.where(row == 2 + i, jnp.sum(tile, axis=0, keepdims=True), stacked)
        if sums.shape == stacked.shape:
            sums[...] = stacked
        else:
            lane = lax.broadcasted_iota(jnp.int32, (8, 128), 1)
            values = jnp.sum(stacked, axis=1, keepdims=True)
            line = jnp.sum(jnp.where(row == lane, values, 0.0), axis=0, keepdims=True)
            sums[...] = jnp.broadcast_to(line[None], sums.shape)

    n = lax.axis_size("dp") * lax.axis_size("shard")
    ends = n_begun or height == prev.shape[1]
    return pl.pallas_call(
        kernel,
        out_shape=(
            jax.ShapeDtypeStruct((1, height, prev.shape[2]), F32),
            jax.ShapeDtypeStruct((n, 1, 128) if ends else (8, 128), F32),
        ),
        in_specs=[VMEM] * (2 + n_arrays + n_lost + n_begun),
        out_specs=(VMEM, VMEM),
        compiler_params=pltpu.CompilerParams(vmem_limit_bytes=12 * MIB),
    )(trig, prev, *arrays.values(), *flat, *begun)


def store(kept):
    shape = (1, sum(x.shape[1] for _, x in kept), kept[0][1].shape[2])

    def kernel(*refs):
        out, sem = refs[len(kept) :]
        copies = []
        for i, (first, x) in enumerate(kept):
            there = pl.ds(first, x.shape[1])
            copies.append(pltpu.make_async_copy(refs[i], out.at[:, there], sem.at[i]))
            copies[-1].start()
        for c in copies:
            c.wait()

    return pl.pallas_call(
        kernel,
        out_shape=jax.ShapeDtypeStruct(shape, F32),
        in_specs=[VMEM] * len(kept),
        out_specs=HBM,
        scratch_shapes=[pltpu.SemaphoreType.DMA((len(kept),))],
        cost_estimate=pl.CostEstimate(flops=0, bytes_accessed=1 << 24, transcendentals=0),
        compiler_params=pltpu.CompilerParams(vmem_limit_bytes=8 * MIB),
        name="store",
    )(*[x for _, x in kept])


def scale(kept, gathered):
    devices = gathered.shape[0]
    shape = (1, sum(x.shape[1] for _, x in kept), kept[0][1].shape[2])
    spans = []
    for i, (first, x) in enumerate(kept):
        step = PIECE if x.shape[1] % PIECE == 0 else BLOCK
        spans += [(i, r, first + r, step) for r in range(0, x.shape[1], step)]

    def kernel(*refs):
        all_ref, out, hits_out, bad_out, buf, hits, bad, sem = refs[len(kept) :]
        table = all_ref[:, 0, :]
        s = jnp.sum(table, axis=0, keepdims=True)
        lane = lax.broadcasted_iota(jnp.int32, (1, 128), 1)
        pick = lambda x, where: jnp.sum(jnp.where(where, x, 0.0), axis=1, keepdims=True)
        square_total = pick(s, lane == 0)
        limit = clip_ratio * jnp.sqrt(jnp.full((1, 1), HID * COLS, F32))
        factor = jnp.minimum(1.0, limit / jnp.sqrt(square_total + epsilon))
        copies = []
        for p, (i, r, first, step) in enumerate(spans):
            there = pl.ds(first, step)
            buf[0, first : first + step, :] = refs[i][0, r : r + step, :] * factor
            copies.append(pltpu.make_async_copy(buf.at[:, there], out.at[:, there], sem.at[p]))
            copies[-1].start()
        most = jnp.max(table, axis=0, keepdims=True)
        n = len(spans)
        hits[...] = pick(s, lane == 1)
        roundings = (lane >= 2) & (lane < 2 + KINDS)
        room = (ROUNDING * ROUNDING / STAGES) * square_total
        over = (pick(s, roundings) > room) | (devices * pick(most, roundings) > 2.0 * room)
        bad[...] = over.astype(jnp.int32)
        copies.append(pltpu.make_async_copy(hits, hits_out, sem.at[n]))
        copies.append(pltpu.make_async_copy(bad, bad_out, sem.at[n + 1]))
        copies[n].start()
        copies[n + 1].start()
        for c in copies:
            c.wait()

    one = lambda t: jax.ShapeDtypeStruct((1, 1), t)
    return pl.pallas_call(
        kernel,
        out_shape=(jax.ShapeDtypeStruct(shape, F32), one(F32), one(jnp.int32)),
        in_specs=[VMEM] * (len(kept) + 1),
        out_specs=(HBM, HBM, HBM),
        scratch_shapes=[
            pltpu.VMEM(shape, F32),
            pltpu.VMEM((1, 1), F32),
            pltpu.VMEM((1, 1), jnp.int32),
            pltpu.SemaphoreType.DMA((len(spans) + 2,)),
        ],
        compiler_params=pltpu.CompilerParams(vmem_limit_bytes=8 * MIB),
        name="scale",
    )(*[x for _, x in kept], gathered)


def local(*args):
    return step(*args)


def step(hidden_acts, out_grad, token_ids, trigger, stale, aggregate_prev):
    n = lax.axis_size("dp")
    chunk = aggregate_prev.shape[1]
    unit = chunk // 16
    args = (trigger, token_ids, hidden_acts, out_grad, stale)

    def swap(x, mask):
        return lax.ppermute(x, "dp", [(i, i ^ mask) for i in range(n)])

    outgoing = [[(m ^ bit, rows) for m, rows in parts] for _, bit, parts in RAW]
    made = list(deltas_first(*args, outgoing[:FIRST], chunk))
    rest = deltas(*args, outgoing[FIRST:] + [[key] for key in OWN_EARLY], chunk)
    made += rest[: len(RAW) - FIRST]
    got = {label: swap(x, bit) for (label, bit, _), x in zip(RAW, made)}
    own = dict(zip(OWN_EARLY, rest[len(RAW) - FIRST :]))
    own.update(zip(OWN_LATE, deltas(*args, [[key] for key in OWN_LATE], chunk)))
    lost = [[] for _ in range(KINDS)]
    for label, bit, mine, others, group in SUMS:
        parts = [(own[mine], 0)] + [(got[name], k * mine[1][1] * unit) for name, k in others]
        total, energy = add_round(parts, mine[1][1] * unit)
        lost[group].append(energy)
        got[label] = swap(total, bit)

    def addends(table):
        pieces = []
        for (first, count), mine, others in table:
            terms = [(own[mine], 0)] + [(got[name], k * count * unit) for name, k in others]
            pieces.append(((first * unit, count * unit), terms))
        return pieces

    kept, sums = total_up(aggregate_prev, addends(FINAL), lost, trigger, ())
    kept_last, sums = total_up(aggregate_prev, addends(LAST), [], trigger, (sums,))
    everyone = lax.all_to_all(sums, ("dp", "shard"), 0, 0, tiled=True)
    kept = [(0, kept_last), (A0[1] * unit, kept)]
    agg = store(kept)
    update, hits, bad = scale(kept, everyone)

    def again(state):
        mine = deltas(*args, [[(m, (0, 16))] for m in range(n)], chunk)
        came = [mine[0]] + [lax.ppermute(mine[m], "dp", [(i, i ^ m) for i in range(n)]) for m in range(1, n)]
        whole = [((0, chunk), [(x, 0) for x in came])]
        new_kept, new_sums = total_up(aggregate_prev, whole, [], trigger, ())
        new_update, _, _ = scale([(0, new_kept)], lax.all_to_all(new_sums, ("dp", "shard"), 0, 0, tiled=True))
        return jnp.zeros((), jnp.int32), new_kept, new_update

    _, agg, update = lax.while_loop(lambda state: state[0] > 0, again, (bad[0, 0], agg, update))
    return agg, update, hits[0, 0]


def exact(hidden_acts, out_grad, token_ids, trigger, stale, aggregate_prev):
    masked = out_grad[0] * (token_ids[0] != 0).astype(BF16)[:, None]
    row_flags = jnp.repeat(trigger[0], BLOCK).astype(F32)[:, None]
    triggered = lax.psum(jnp.sum(trigger.astype(F32)), ("dp", "shard"))
    gradient = lax.dot_general(hidden_acts[0], masked, (((0,), (0,)), ((), ())), preferred_element_type=F32)
    delta = (row_flags * (gradient - stale[0].astype(F32))).astype(BF16)
    delta = delta.reshape(lax.axis_size("dp"), aggregate_prev.shape[1], stale.shape[2])
    received = lax.all_to_all(delta, "dp", split_axis=0, concat_axis=0, tiled=True)
    aggregate = aggregate_prev[0] + jnp.sum(received, axis=0, dtype=F32)
    square_total = lax.psum(jnp.sum(aggregate * aggregate), ("dp", "shard"))
    limit = clip_ratio * jnp.sqrt(jnp.asarray(HID * COLS, F32))
    factor = jnp.minimum(1.0, limit / jnp.sqrt(square_total + epsilon))
    return aggregate[None], (aggregate * factor)[None], triggered


def solution(mesh):
    staged = mesh.shape["dp"] == 8
    return jax.shard_map(
        local if staged else exact,
        mesh=mesh,
        in_specs=(
            P("dp", None, "shard"),
            P("dp", None, None),
            P("dp", None),
            P("dp", "shard"),
            P("dp", "shard", None),
            P("shard", "dp", None),
        ),
        out_specs=(P("shard", "dp", None), P("shard", "dp", None), P()),
        check_vma=False,
    )
```

```python
import jax
import jax.numpy as jnp
from jax import lax
from jax.experimental import pallas as pl
from jax.experimental.pallas import tpu as pltpu
from jax.sharding import PartitionSpec as P

COLS = 1024
HID = 8192
BLOCK = 16
clip_ratio = 0.25
epsilon = 1e-06
MIB = 1 << 20
PIECE = 32
STAGES = 3
KINDS = 6
ROUNDING = 4.8e-4
F32, BF16 = jnp.float32, jnp.bfloat16
VMEM = pl.BlockSpec(memory_space=pltpu.VMEM)
SMEM = pl.BlockSpec(memory_space=pltpu.SMEM)
HBM = pl.BlockSpec(memory_space=pltpu.HBM)

A0, A1, B = (6, 6), (0, 6), (12, 4)
RAW = (
    ("y6a", 1, ((6, A0),)),
    ("zb0", 2, ((5, B), (4, B))),
    ("y4a", 1, ((4, A0),)),
    ("y6b", 1, ((6, A1),)),
    ("zb1", 2, ((1, B), (0, B))),
    ("y4b", 1, ((4, A1),)),
    ("y2a", 1, ((2, A0),)),
    ("y2b", 1, ((2, A1),)),
    ("y0b", 1, ((0, A1),)),
    ("y0a", 1, ((0, A0),)),
)
FIRST = 2
OWN_EARLY = ((6, A0), (5, B), (4, A0), (6, A1))
OWN_LATE = ((4, B), (4, A1), (1, B), (2, A0), (2, A1), (0, A0), (0, A1), (0, B))
SUMS = (
    ("near0", 2, (6, A0), (("y6a", 0),), 0),
    ("pairb5", 1, (5, B), (("zb0", 0),), 3),
    ("quad0", 4, (4, A0), (("y4a", 0), ("near0", 0)), 1),
    ("near1", 2, (6, A1), (("y6b", 0),), 0),
    ("pairb1", 1, (1, B), (("zb1", 0),), 5),
    ("quadb", 4, (4, B), (("zb0", 1), ("pairb5", 0)), 4),
    ("quad1", 4, (4, A1), (("y4b", 0), ("near1", 0)), 1),
    ("last0", 2, (2, A0), (("y2a", 0),), 2),
    ("last1", 2, (2, A1), (("y2b", 0),), 2),
)
FINAL = (
    (B, (0, B), (("zb1", 1), ("pairb1", 0), ("quadb", 0))),
    (A0, (0, A0), (("y0a", 0), ("last0", 0), ("quad0", 0))),
)
LAST = ((A1, (0, A1), (("y0b", 0), ("last1", 0), ("quad1", 0))),)


def fold(x):
    sq = x * x
    total = jnp.zeros((8, 128), F32)
    for c in range(0, x.shape[1], 128):
        for r in range(0, x.shape[0], 8):
            total = total + sq[r : r + 8, c : c + 128]
    return total


def plan(messages, chunk):
    unit = chunk // 16
    pieces, heights = [], []
    for i, message in enumerate(messages):
        at = 0
        for mask, (first, count) in message:
            pieces.append((i, at, mask, first * unit, count * unit))
            at += count * unit
        heights.append(at)
    return pieces, list(dict.fromkeys(p[2] for p in pieces)), heights


def piece_rows(weights, og, old, trig_ref, block, out):
    gradient = jnp.dot(weights, og, preferred_element_type=F32)
    for b in range(0, gradient.shape[0], BLOCK):
        flag = trig_ref[0, block + b // BLOCK].astype(F32)
        out[b : b + BLOCK, :] = (flag * (gradient[b : b + BLOCK] - old(b).astype(F32))).astype(BF16)


def deltas_first(trig, tok, acts, og, stale, messages, chunk):
    tokens, width = og.shape[1], og.shape[2]
    pieces, masks, heights = plan(messages, chunk)
    total, n_out = sum(heights), len(messages)

    def kernel(trig_hbm, tok_hbm, acts_hbm, og_hbm, stale_hbm, *refs):
        outs = refs[:n_out]
        acts_buf, og_buf, stale_buf, tok_ref, trig_ref, sem = refs[n_out : n_out + 6]
        me = lax.axis_index("dp")
        start = {m: pl.multiple_of((me ^ m) * chunk, chunk) for m in masks}
        sems = iter(range(3 + len(masks) + len(pieces)))
        begin = lambda source, target: pltpu.make_async_copy(source, target, sem.at[next(sems)])
        acts_of = lambda j: begin(acts_hbm.at[0, :, pl.ds(start[masks[j]], chunk)], acts_buf.at[j])
        first_acts, og_copy = acts_of(0), begin(og_hbm.at[0], og_buf)
        tok_copy, trig_copy = begin(tok_hbm, tok_ref), begin(trig_hbm, trig_ref)
        stale_copies, at = [], 0
        for _, _, m, first, rows in pieces:
            source = stale_hbm.at[0, pl.ds(pl.multiple_of(start[m] + first, BLOCK), rows), :]
            stale_copies.append(begin(source, stale_buf.at[pl.ds(at, rows), :]))
            at += rows
        act_copies = [first_acts] + [acts_of(j) for j in range(1, len(masks))]
        for copy in [first_acts, og_copy, stale_copies[0], tok_copy, trig_copy] + act_copies[1:] + stale_copies[1:]:
            copy.start()
        tok_copy.wait()
        trig_copy.wait()
        real = (tok_ref[...] != 0).astype(BF16)
        weights, at = {}, 0
        for j, (i, offset, m, first, rows) in enumerate(pieces):
            if m not in weights:
                act_copies[masks.index(m)].wait()
                weights[m] = acts_buf[masks.index(m)].T * real
            if j == 0:
                og_copy.wait()
            stale_copies[j].wait()
            old = lambda b, at=at: stale_buf[at + b : at + b + BLOCK, :]
            block = (start[m] + first) // BLOCK
            piece_rows(
                weights[m][first : first + rows], og_buf[...], old, trig_ref, block, outs[i].at[pl.ds(offset, rows), :]
            )
            at += rows

    return pl.pallas_call(
        kernel,
        out_shape=tuple(jax.ShapeDtypeStruct((h, width), BF16) for h in heights),
        in_specs=[HBM] * 5,
        out_specs=tuple(VMEM for _ in messages),
        scratch_shapes=[
            pltpu.VMEM((len(masks), tokens, chunk), BF16),
            pltpu.VMEM((tokens, width), BF16),
            pltpu.VMEM((total, width), BF16),
            pltpu.VMEM(tok.shape, jnp.int32),
            pltpu.SMEM(trig.shape, jnp.int32),
            pltpu.SemaphoreType.DMA((4 + len(masks) + len(pieces),)),
        ],
        cost_estimate=pl.CostEstimate(
            flops=2 * tokens * total * width, bytes_accessed=total * width * 4, transcendentals=0
        ),
        compiler_params=pltpu.CompilerParams(vmem_limit_bytes=16 * MIB),
    )(trig, tok, acts, og, stale)


def deltas(trig, tok, acts, og, stale, messages, chunk):
    tokens, width = og.shape[1], og.shape[2]
    pieces, masks, heights = plan(messages, chunk)

    def kernel(trig_hbm, tok_ref, acts_ref, og_ref, stale_ref, *refs):
        outs, (trig_ref, sem) = refs[:-2], refs[-2:]
        trig_copy = pltpu.make_async_copy(trig_hbm, trig_ref, sem.at[0])
        trig_copy.start()
        me = lax.axis_index("dp")
        start = {m: pl.multiple_of((me ^ m) * chunk, chunk) for m in masks}
        real = (tok_ref[...] != 0).astype(BF16)
        weights = {}
        for j, (i, offset, m, first, rows) in enumerate(pieces):
            if m not in weights:
                weights[m] = acts_ref[0, :, pl.ds(start[m], chunk)].T * real
            if j == 0:
                trig_copy.wait()
            old = lambda b, m=m, first=first: stale_ref[0, pl.ds(pl.multiple_of(start[m] + first + b, BLOCK), BLOCK), :]
            block = (start[m] + first) // BLOCK
            piece_rows(
                weights[m][first : first + rows], og_ref[0], old, trig_ref, block, outs[i].at[pl.ds(offset, rows), :]
            )

    total = sum(heights)
    return pl.pallas_call(
        kernel,
        out_shape=tuple(jax.ShapeDtypeStruct((h, width), BF16) for h in heights),
        in_specs=[HBM] + [VMEM] * 4,
        out_specs=tuple(VMEM for _ in messages),
        scratch_shapes=[pltpu.SMEM(trig.shape, jnp.int32), pltpu.SemaphoreType.DMA((1,))],
        cost_estimate=pl.CostEstimate(
            flops=2 * tokens * total * width, bytes_accessed=total * width * 4, transcendentals=0
        ),
        compiler_params=pltpu.CompilerParams(vmem_limit_bytes=16 * MIB),
    )(trig, tok, acts, og, stale)


def add_round(parts, rows):
    width = parts[0][0].shape[1]

    def kernel(*refs):
        out, lost = refs[-2:]
        energy = jnp.zeros((8, 128), F32)
        for r in range(0, rows, BLOCK):
            total = jnp.zeros((BLOCK, width), F32)
            for ref, (_, at) in zip(refs, parts):
                total = total + ref[at + r : at + r + BLOCK, :].astype(F32)
            rounded = total.astype(BF16)
            out[r : r + BLOCK, :] = rounded
            energy = energy + fold(total - rounded.astype(F32))
        lost[...] = energy

    return pl.pallas_call(
        kernel,
        out_shape=(jax.ShapeDtypeStruct((rows, width), BF16), jax.ShapeDtypeStruct((8, 128), F32)),
        in_specs=[VMEM] * len(parts),
        out_specs=(VMEM, VMEM),
        cost_estimate=pl.CostEstimate(flops=rows * width * 6, bytes_accessed=rows * width * 6, transcendentals=0),
        compiler_params=pltpu.CompilerParams(vmem_limit_bytes=12 * MIB),
    )(*[x for x, _ in parts])


def total_up(prev, groups, lost, trig, begun):
    arrays = {id(x): x for _, addends in groups for x, _ in addends}
    keys = list(arrays)
    flat = [x for group in lost for x in group]
    n_arrays, n_lost, n_begun = len(keys), len(flat), len(begun)
    lowest = min(first for (first, _), _ in groups)
    height = sum(rows for (_, rows), _ in groups)

    def kernel(trig_ref, prev_ref, *refs):
        lost_refs = list(refs[n_arrays : n_arrays + n_lost])
        before = refs[n_arrays + n_lost :][:n_begun]
        kept, sums = refs[n_arrays + n_lost + n_begun :]
        total = jnp.zeros((8, 128), F32)
        for (first, rows), addends in groups:
            for r in range(0, rows, BLOCK):
                a = prev_ref[0, first + r : first + r + BLOCK, :]
                for x, at in addends:
                    a = a + refs[keys.index(id(x))][at + r : at + r + BLOCK, :].astype(F32)
                kept[0, first - lowest + r : first - lowest + r + BLOCK, :] = a
                total = total + fold(a)
        row = lax.broadcasted_iota(jnp.int32, (8, 128), 0)
        if n_begun:
            stacked = before[0][...]
        else:
            stacked = jnp.where(row == 1, trig_ref[...].astype(F32), 0.0)
        stacked = stacked + jnp.where(row == 0, jnp.sum(total, axis=0, keepdims=True), 0.0)
        for i, group in enumerate(lost):
            tile = sum(lost_refs.pop(0)[...] for _ in group)
            stacked = jnp.where(row == 2 + i, jnp.sum(tile, axis=0, keepdims=True), stacked)
        if sums.shape == stacked.shape:
            sums[...] = stacked
        else:
            lane = lax.broadcasted_iota(jnp.int32, (8, 128), 1)
            values = jnp.sum(stacked, axis=1, keepdims=True)
            line = jnp.sum(jnp.where(row == lane, values, 0.0), axis=0, keepdims=True)
            sums[...] = jnp.broadcast_to(line[None], sums.shape)

    n = lax.axis_size("dp") * lax.axis_size("shard")
    ends = n_begun or height == prev.shape[1]
    return pl.pallas_call(
        kernel,
        out_shape=(
            jax.ShapeDtypeStruct((1, height, prev.shape[2]), F32),
            jax.ShapeDtypeStruct((n, 1, 128) if ends else (8, 128), F32),
        ),
        in_specs=[VMEM] * (2 + n_arrays + n_lost + n_begun),
        out_specs=(VMEM, VMEM),
        compiler_params=pltpu.CompilerParams(vmem_limit_bytes=12 * MIB),
    )(trig, prev, *arrays.values(), *flat, *begun)


def store(kept):
    shape = (1, sum(x.shape[1] for _, x in kept), kept[0][1].shape[2])

    def kernel(*refs):
        out, sem = refs[len(kept) :]
        copies = []
        for i, (first, x) in enumerate(kept):
            there = pl.ds(first, x.shape[1])
            copies.append(pltpu.make_async_copy(refs[i], out.at[:, there], sem.at[i]))
            copies[-1].start()
        for c in copies:
            c.wait()

    return pl.pallas_call(
        kernel,
        out_shape=jax.ShapeDtypeStruct(shape, F32),
        in_specs=[VMEM] * len(kept),
        out_specs=HBM,
        scratch_shapes=[pltpu.SemaphoreType.DMA((len(kept),))],
        cost_estimate=pl.CostEstimate(flops=0, bytes_accessed=1 << 24, transcendentals=0),
        compiler_params=pltpu.CompilerParams(vmem_limit_bytes=8 * MIB),
        name="store",
    )(*[x for _, x in kept])


def scale(kept, gathered):
    devices = gathered.shape[0]
    shape = (1, sum(x.shape[1] for _, x in kept), kept[0][1].shape[2])
    spans = []
    for i, (first, x) in enumerate(kept):
        step = PIECE if x.shape[1] % PIECE == 0 else BLOCK
        spans += [(i, r, first + r, step) for r in range(0, x.shape[1], step)]

    def kernel(*refs):
        all_ref, out, hits_out, bad_out, buf, hits, bad, sem = refs[len(kept) :]
        table = all_ref[:, 0, :]
        s = jnp.sum(table, axis=0, keepdims=True)
        lane = lax.broadcasted_iota(jnp.int32, (1, 128), 1)
        pick = lambda x, where: jnp.sum(jnp.where(where, x, 0.0), axis=1, keepdims=True)
        square_total = pick(s, lane == 0)
        limit = clip_ratio * jnp.sqrt(jnp.full((1, 1), HID * COLS, F32))
        factor = jnp.minimum(1.0, limit / jnp.sqrt(square_total + epsilon))
        copies = []
        for p, (i, r, first, step) in enumerate(spans):
            there = pl.ds(first, step)
            buf[0, first : first + step, :] = refs[i][0, r : r + step, :] * factor
            copies.append(pltpu.make_async_copy(buf.at[:, there], out.at[:, there], sem.at[p]))
            copies[-1].start()
        most = jnp.max(table, axis=0, keepdims=True)
        n = len(spans)
        hits[...] = pick(s, lane == 1)
        roundings = (lane >= 2) & (lane < 2 + KINDS)
        room = (ROUNDING * ROUNDING / STAGES) * square_total
        over = (pick(s, roundings) > room) | (devices * pick(most, roundings) > 2.0 * room)
        bad[...] = over.astype(jnp.int32)
        copies.append(pltpu.make_async_copy(hits, hits_out, sem.at[n]))
        copies.append(pltpu.make_async_copy(bad, bad_out, sem.at[n + 1]))
        copies[n].start()
        copies[n + 1].start()
        for c in copies:
            c.wait()

    one = lambda t: jax.ShapeDtypeStruct((1, 1), t)
    return pl.pallas_call(
        kernel,
        out_shape=(jax.ShapeDtypeStruct(shape, F32), one(F32), one(jnp.int32)),
        in_specs=[VMEM] * (len(kept) + 1),
        out_specs=(HBM, HBM, HBM),
        scratch_shapes=[
            pltpu.VMEM(shape, F32),
            pltpu.VMEM((1, 1), F32),
            pltpu.VMEM((1, 1), jnp.int32),
            pltpu.SemaphoreType.DMA((len(spans) + 2,)),
        ],
        compiler_params=pltpu.CompilerParams(vmem_limit_bytes=8 * MIB),
        name="scale",
    )(*[x for _, x in kept], gathered)


def local(*args):
    return step(*args)


def step(hidden_acts, out_grad, token_ids, trigger, stale, aggregate_prev):
    n = lax.axis_size("dp")
    chunk = aggregate_prev.shape[1]
    unit = chunk // 16
    args = (trigger, token_ids, hidden_acts, out_grad, stale)

    def swap(x, mask):
        return lax.ppermute(x, "dp", [(i, i ^ mask) for i in range(n)])

    outgoing = [[(m ^ bit, rows) for m, rows in parts] for _, bit, parts in RAW]
    made = list(deltas_first(*args, outgoing[:FIRST], chunk))
    rest = deltas(*args, outgoing[FIRST:] + [[key] for key in OWN_EARLY], chunk)
    made += rest[: len(RAW) - FIRST]
    got = {label: swap(x, bit) for (label, bit, _), x in zip(RAW, made)}
    own = dict(zip(OWN_EARLY, rest[len(RAW) - FIRST :]))
    own.update(zip(OWN_LATE, deltas(*args, [[key] for key in OWN_LATE], chunk)))
    lost = [[] for _ in range(KINDS)]
    for label, bit, mine, others, group in SUMS:
        parts = [(own[mine], 0)] + [(got[name], k * mine[1][1] * unit) for name, k in others]
        total, energy = add_round(parts, mine[1][1] * unit)
        lost[group].append(energy)
        got[label] = swap(total, bit)

    def addends(table):
        pieces = []
        for (first, count), mine, others in table:
            terms = [(own[mine], 0)] + [(got[name], k * count * unit) for name, k in others]
            pieces.append(((first * unit, count * unit), terms))
        return pieces

    kept, sums = total_up(aggregate_prev, addends(FINAL), lost, trigger, ())
    kept_last, sums = total_up(aggregate_prev, addends(LAST), [], trigger, (sums,))
    everyone = lax.all_to_all(sums, ("dp", "shard"), 0, 0, tiled=True)
    kept = [(0, kept_last), (A1[1] * unit, kept)]
    agg = store(kept)
    update, hits, bad = scale(kept, everyone)

    def again(state):
        mine = deltas(*args, [[(m, (0, 16))] for m in range(n)], chunk)
        came = [mine[0]] + [lax.ppermute(mine[m], "dp", [(i, i ^ m) for i in range(n)]) for m in range(1, n)]
        whole = [((0, chunk), [(x, 0) for x in came])]
        new_kept, new_sums = total_up(aggregate_prev, whole, [], trigger, ())
        new_update, _, _ = scale([(0, new_kept)], lax.all_to_all(new_sums, ("dp", "shard"), 0, 0, tiled=True))
        return jnp.zeros((), jnp.int32), new_kept, new_update

    _, agg, update = lax.while_loop(lambda state: state[0] > 0, again, (bad[0, 0], agg, update))
    return agg, update, hits[0, 0]


def exact(hidden_acts, out_grad, token_ids, trigger, stale, aggregate_prev):
    masked = out_grad[0] * (token_ids[0] != 0).astype(BF16)[:, None]
    row_flags = jnp.repeat(trigger[0], BLOCK).astype(F32)[:, None]
    triggered = lax.psum(jnp.sum(trigger.astype(F32)), ("dp", "shard"))
    gradient = lax.dot_general(hidden_acts[0], masked, (((0,), (0,)), ((), ())), preferred_element_type=F32)
    delta = (row_flags * (gradient - stale[0].astype(F32))).astype(BF16)
    delta = delta.reshape(lax.axis_size("dp"), aggregate_prev.shape[1], stale.shape[2])
    received = lax.all_to_all(delta, "dp", split_axis=0, concat_axis=0, tiled=True)
    aggregate = aggregate_prev[0] + jnp.sum(received, axis=0, dtype=F32)
    square_total = lax.psum(jnp.sum(aggregate * aggregate), ("dp", "shard"))
    limit = clip_ratio * jnp.sqrt(jnp.asarray(HID * COLS, F32))
    factor = jnp.minimum(1.0, limit / jnp.sqrt(square_total + epsilon))
    return aggregate[None], (aggregate * factor)[None], triggered


def solution(mesh):
    staged = mesh.shape["dp"] == 8
    return jax.shard_map(
        local if staged else exact,
        mesh=mesh,
        in_specs=(
            P("dp", None, "shard"),
            P("dp", None, None),
            P("dp", None),
            P("dp", "shard"),
            P("dp", "shard", None),
            P("shard", "dp", None),
        ),
        out_specs=(P("shard", "dp", None), P("shard", "dp", None), P()),
        check_vma=False,
    )
```
